32 devices in a mesh: shots: 2 (over y), tx: 16 (over z, x, core).
Axes of the slice: x: 2, y: 2, z: 4, core: 2. Of those that a mesh axis runs over, the one named last changes fastest.
Arguments:
- kappa: float32 [32, 128, 128], P('tx'), may hold values from 1 to 4
- buoyancy: float32 [32, 128, 128], P('tx'), may hold values from 0.5 to 1.5
- source_state: float32 [4, 64, 128, 128], P(None, ('shots', 'tx')), parts along dimension 1, may hold values from -6 to 6
- traces: float32 [512, 12, 128], P(('shots', 'tx')), parts along dimension 0, may hold values from -6 to 6
- panel_tile: int32 [512, 1], P(('shots', 'tx')), parts along dimension 0, may hold values from 0 to 15; in each aligned block of 16 rows (0 to 15, 16 to 31, ...) at most 2 rows name the same one
- rcv_index: int32 [512, 128], P(('shots', 'tx')), parts along dimension 0, may hold values from 0 to 32767
Outputs:
- image: float32 [64, 128, 128], P(('shots', 'tx')), parts along dimension 0
- receiver_pressure: float32 [64, 128, 128], P(('shots', 'tx')), parts along dimension 0
The draws below stay inside these ranges and needn't reach their ends.
There are 2 independent parts, one for each index of `shots`. The reference program is written for one: setup_inputs(seed, part) draws one part's arguments, and reference() takes and returns one part's arrays. A program takes and returns all parts, laid end to end along the dimension named above; an argument that names none is the same for every part. Nothing has to cross between parts.
Inputs may be any that keep to these rules, and one draw needn't show every extreme that they name: `panel_tile`: in the rows of one tile, no tile is named by more than 2 panels, a bound that some block reaches. `rcv_index`: the flat index x * 128 * 128 + y * 128 + z of a cell within the panel's tile.
All inputs are finite; a program needn't handle non-finite values.
Results may differ from the reference program's by a relative error of at most 0.0001.
Values sent between devices are 32-bit elements; how exact they have to be, the bound alone decides.
A program may use at most 128 MiB of HBM per device.

```python
import math
import jax
import jax.numpy as jnp
import numpy as np
from jax import lax

CX = 2
NY = 128
NZ = 128
STEPS = 12
RCV = 128
CAP = 2
PAN = 16
NX = 32
PANELS = 256
N_TX = 16


def draw_source_state(key, part):
    first_key = jax.random.fold_in(jax.random.fold_in(key, 17), 0)
    base = jax.random.normal(first_key, (4, NX, NY, NZ), jnp.float32)
    values = base
    return jnp.clip(values, -6.0, 6.0)


def plant(values, rng, low, largest):
    spot = [jax.random.randint(jax.random.fold_in(rng, axis), (), 0, length) for axis, length in enumerate(values.shape)]
    main_axis = values.shape.index(max(values.shape))
    neighbour = spot[:main_axis] + [(spot[main_axis] + 1) % values.shape[main_axis]] + spot[main_axis + 1:]
    return values.at[tuple(spot)].set(low).at[tuple(neighbour)].set(largest)


def steps_of(stream_key, shape, pieces, least, largest):
    factor_of, own = 1.0, jax.random.fold_in(stream_key, 6)
    for dim, parts in pieces:
        heights = jnp.exp(jax.random.uniform(jax.random.fold_in(own, dim), (parts,), jnp.float32, least / len(pieces), largest / len(pieces)))
        factor_of = factor_of * jnp.repeat(heights, shape[dim] // parts).reshape([-1 if axis == dim else 1 for axis in range(len(shape))])
    return factor_of


def deal_out(rng, own, number, rows, count, top, bound, slope):
    sequence = jax.random.permutation(rng, count)
    crowded, usual = shares(count, rows * top, bound, slope, True), shares(count, rows * top, bound, slope, False)
    places = jnp.arange(count)

    def named(sizes, offset_by):
        used = int((sizes > 0).sum())
        fixed = max(1, used // 4)
        shifted = fixed + (places - fixed + offset_by * (used - fixed)) % max(1, count - fixed)
        return jnp.zeros((count,), jnp.int32).at[sequence[jnp.where(places < fixed, places, shifted)]].set(jnp.asarray(sizes, jnp.int32))

    sizes = jnp.where(number % 4 == 0, named(crowded, number // 4), named(usual, number - number // 4 - 1))
    mixed = jax.random.permutation(jax.random.fold_in(own, 3), count)
    donor, taker = mixed[0:count // 2 * 2:2], mixed[1:count // 2 * 2:2]
    room = jnp.minimum(sizes[donor] - 1, bound - sizes[taker]) // 2
    room = jnp.where((donor == sequence[0]) | (taker == sequence[0]) | (sizes[taker] == 0), 0, jnp.maximum(room, 0))
    shifted = jax.random.randint(jax.random.fold_in(own, 4), (count // 2,), 0, 1 << 20) % (room + 1)
    sizes = sizes.at[donor].add(-shifted).at[taker].add(shifted)
    members = jnp.searchsorted(jnp.cumsum(sizes), jnp.arange(rows * top), side="right").astype(jnp.int32)
    table = members.reshape(top, rows).T
    table = table[jax.random.permutation(jax.random.fold_in(own, 1), rows)]
    offset_by = jax.random.randint(jax.random.fold_in(own, 2), (rows, 1), 0, top)
    return jnp.take_along_axis(table, (jnp.arange(top)[None, :] + offset_by) % top, axis=1)


def shares(count, total, reach, lean, full):
    loads = [(1 << 20) // math.isqrt(rank ** lean) + 1 for rank in range(1, count + 1)]
    largest = reach if full else min(reach, max(-(-total // count), total * loads[0] // sum(loads)))
    least = 1 if total - largest >= count - 1 else 0
    counts, surplus = [largest] + [least] * (count - 1), total - largest - least * (count - 1)
    while surplus > 0:
        free = [i for i in range(1, count) if counts[i] < largest] or [i for i in range(1, count) if counts[i] < reach]
        whole, remaining = sum([loads[i] for i in free]), surplus
        for i in free:
            addition = min(reach - counts[i], max(1, remaining * loads[i] // whole), surplus)
            counts[i] = counts[i] + addition
            surplus = surplus - addition
    return np.array(counts)


def centred(rng, dims, width, most, cuts=(), kind=jnp.bfloat16):
    result = jax.random.normal(rng, dims, jnp.float32) * width
    if len(cuts) > 0:
        result = steps_of(rng, dims, cuts, -0.22, 0.18) * result
    return jnp.clip(result, min=-most, max=most).astype(kind)


def setup_inputs(seed: int = 0, part: int = 0) -> dict:
    seeds = jax.random.split(jax.random.key(seed), 7)
    part_splits = jax.random.split(jax.random.fold_in(seeds[6], part), 7)
    kappa = jnp.clip(jnp.exp(math.log(4.0) - 1.3862944 * jax.random.uniform(seeds[0], (NX, NY, NZ), jnp.float32) ** steps_of(seeds[0], (NX, NY, NZ), ((0, 16),), -0.2, 0.2)), 1.0, 4.0)
    buoyancy = jnp.clip(jnp.exp(math.log(1.5) - 1.0986123 * jax.random.uniform(seeds[1], (NX, NY, NZ), jnp.float32) ** steps_of(seeds[1], (NX, NY, NZ), ((0, 16),), -0.2, 0.2)), 0.5, 1.5)
    source_state = draw_source_state(jax.random.fold_in(jax.random.fold_in(seeds[6], part), 71), part)
    traces = centred(part_splits[3], (PANELS, STEPS, RCV), 1.0, 6.0, ((0, 16),), jnp.float32)
    panel_tile_keys = jax.random.split(jax.random.fold_in(part_splits[4], 1), PANELS // PAN)
    panel_tile_turns = jax.random.permutation(jax.random.fold_in(part_splits[4], 3), PANELS // PAN)
    panel_tile = jax.vmap(lambda own, number: deal_out(jax.random.fold_in(part_splits[4], 2), own, number, PAN, N_TX, 1, CAP, 2))(panel_tile_keys, panel_tile_turns).reshape((PANELS, 1))
    rcv_index = plant(jax.random.randint(part_splits[5], (PANELS, RCV), 0, CX * NY * NZ), jax.random.fold_in(part_splits[5], 1), 0, (CX * NY * NZ) - 1).astype(jnp.int32)
    return {"kappa": kappa, "buoyancy": buoyancy, "source_state": source_state, "traces": traces, "panel_tile": panel_tile, "rcv_index": rcv_index}


COEFS = (1225.0 / 1024.0, -245.0 / 3072.0, 49.0 / 5120.0, -5.0 / 7168.0)
TIME_STEP = 0.15


def window(array, start, count, axis):
    return lax.slice_in_dim(array, start, start + count, axis=axis)


def forward_diff(padded, axis, start, count):
    total = jnp.zeros_like(window(padded, start, count, axis))
    for order in range(1, 5):
        total = total + COEFS[order - 1] * (window(padded, start + order, count, axis) - window(padded, start - order + 1, count, axis))
    return total


def backward_diff(padded, axis, start, count):
    total = jnp.zeros_like(window(padded, start, count, axis))
    for order in range(1, 5):
        total = total + COEFS[order - 1] * (window(padded, start + order - 1, count, axis) - window(padded, start - order, count, axis))
    return total


def pad_axis(array, axis):
    widths = [(0, 0)] * array.ndim
    widths[axis] = (4, 4)
    return jnp.pad(array, widths)


def spectral_table(count, offset):
    row_ids = jnp.arange(count, dtype=jnp.int32)[:, None]
    col_ids = jnp.arange(count, dtype=jnp.int32)[None, :]
    shift = col_ids - row_ids + offset
    sign = (1 - 2 * ((shift + 1) % 2)).astype(jnp.float32)
    odd = (2 * shift - 1).astype(jnp.float32)
    return sign * (4.0 / math.pi) / (odd * odd)


def along_x(table, field):
    return jnp.einsum("ij,wjyz->wiyz", table, field, precision=lax.Precision.HIGHEST)


def reference(kappa, buoyancy, source_state, traces, panel_tile, rcv_index):
    cells = CX * NY * NZ
    zeros = jnp.zeros_like(source_state[0])
    pres = jnp.stack([source_state[0], zeros])
    velx = jnp.stack([source_state[1], zeros])
    vely = jnp.stack([source_state[2], zeros])
    velz = jnp.stack([source_state[3], zeros])
    flat_index = (panel_tile[:, 0:1].astype(jnp.int32) * cells + rcv_index.astype(jnp.int32)).reshape(-1)
    image = zeros
    nx = pres.shape[1]
    forward_table = spectral_table(nx, 0)
    backward_table = spectral_table(nx, 1)
    for step in range(STEPS):
        velx = velx - TIME_STEP * buoyancy * along_x(forward_table, pres)
        vely = vely - TIME_STEP * buoyancy * forward_diff(pad_axis(pres, 2), 2, 4, NY)
        velz = velz - TIME_STEP * buoyancy * forward_diff(pad_axis(pres, 3), 3, 4, NZ)
        diverge = along_x(backward_table, velx)
        diverge = diverge + backward_diff(pad_axis(vely, 2), 2, 4, NY)
        diverge = diverge + backward_diff(pad_axis(velz, 3), 3, 4, NZ)
        pres = pres - TIME_STEP * kappa * diverge
        source_term = jnp.zeros((nx * NY * NZ,), jnp.float32).at[flat_index].add(TIME_STEP * traces[:, step, :].reshape(-1))
        pres = pres.at[1].add(source_term.reshape(nx, NY, NZ))
        image = image + pres[0] * pres[1]
    return image, pres[1]
```

```python
import math

import jax
import jax.numpy as jnp
import numpy as np
from jax import lax
from jax.experimental import pallas as pl
from jax.experimental.pallas import tpu as pltpu
from jax.sharding import PartitionSpec as P

CAP = 2


COEFS = (1225.0 / 1024.0, -245.0 / 3072.0, 49.0 / 5120.0, -5.0 / 7168.0)
TIME_STEP = 0.15


def window(array, start, count, axis):
    return lax.slice_in_dim(array, start, start + count, axis=axis)


def forward_diff(padded, axis, start, count):
    total = jnp.zeros_like(window(padded, start, count, axis))
    for order in range(1, 5):
        total = total + COEFS[order - 1] * (
            window(padded, start + order, count, axis)
            - window(padded, start - order + 1, count, axis)
        )
    return total


def backward_diff(padded, axis, start, count):
    total = jnp.zeros_like(window(padded, start, count, axis))
    for order in range(1, 5):
        total = total + COEFS[order - 1] * (
            window(padded, start + order - 1, count, axis)
            - window(padded, start - order, count, axis)
        )
    return total


def pad_axis(array, axis):
    widths = [(0, 0)] * array.ndim
    widths[axis] = (4, 4)
    return jnp.pad(array, widths)


def spectral_table(count, offset):
    row_ids = jnp.arange(count, dtype=jnp.int32)[:, None]
    col_ids = jnp.arange(count, dtype=jnp.int32)[None, :]
    shift = col_ids - row_ids + offset
    sign = (1 - 2 * ((shift + 1) % 2)).astype(jnp.float32)
    odd = (2 * shift - 1).astype(jnp.float32)
    return sign * (4.0 / math.pi) / (odd * odd)


def along_lines(table, lines):
    return jnp.einsum("ij,wjkc->wikc", table, lines, precision=lax.Precision.HIGHEST)


def transposed_path(kappa, buoyancy, source_state, traces, panel_tile, rcv_index):
    count = kappa.shape[0]
    depth_y = kappa.shape[1]
    depth_z = kappa.shape[2]
    tiles = lax.axis_size("tx")
    columns = depth_y * depth_z // tiles
    extent = count * tiles
    forward_table = spectral_table(extent, 0)
    backward_table = spectral_table(extent, 1)
    panels = traces.shape[0]
    samples_count = traces.shape[1]
    receivers = traces.shape[2]
    dest = panel_tile[:, 0]
    same = dest[:, None] == dest[None, :]
    earlier = jnp.arange(panels)[None, :] < jnp.arange(panels)[:, None]
    rank = jnp.sum((same & earlier).astype(jnp.int32), axis=1)
    target = dest * CAP + rank
    onehot = (target[:, None] == jnp.arange(tiles * CAP)[None, :]).astype(jnp.float32)
    payload = jnp.concatenate([rcv_index.astype(jnp.float32)[:, None, :], traces], axis=1).reshape(
        panels, -1
    )
    packed = lax.dot_general(
        onehot, payload, (((0,), (0,)), ((), ())), precision=lax.Precision.HIGHEST
    )
    packed = packed.reshape(tiles, CAP, (samples_count + 1) * receivers)
    arrived = lax.all_to_all(packed, "tx", split_axis=0, concat_axis=0, tiled=True).reshape(
        tiles * CAP, samples_count + 1, receivers
    )
    local_index = arrived[:, 0, :].astype(jnp.int32).reshape(-1)
    samples = arrived[:, 1:, :]
    sample_rows = TIME_STEP * jnp.transpose(samples, (0, 2, 1)).reshape(-1, samples_count)
    dense = (
        jnp.zeros((count * depth_y * depth_z, samples_count), jnp.float32)
        .at[local_index]
        .add(sample_rows)
    )
    sources = jnp.transpose(dense).reshape(samples_count, count, depth_y, depth_z)

    def to_lines(field):
        return field.reshape(field.shape[0], count, tiles, columns)

    def from_lines(field):
        return field.reshape(field.shape[0], count, depth_y, depth_z)

    def gradient_home(lines):
        return lax.all_to_all(
            along_lines(forward_table, lines), "tx", split_axis=1, concat_axis=2, tiled=True
        )

    def divergence_home(lines):
        return lax.all_to_all(
            along_lines(backward_table, lines), "tx", split_axis=1, concat_axis=2, tiled=True
        )

    zeros = jnp.zeros_like(source_state[0])
    pres = jnp.stack([source_state[0], zeros])
    velx = jnp.stack([source_state[1], zeros])
    vely = jnp.stack([source_state[2], zeros])
    velz = jnp.stack([source_state[3], zeros])
    velx_state = velx

    def advance(step, carry):
        pres, velx_state, vely, velz, image = carry
        vely = vely - TIME_STEP * buoyancy * forward_diff(pad_axis(pres, 2), 2, 4, depth_y)
        velz = velz - TIME_STEP * buoyancy * forward_diff(pad_axis(pres, 3), 3, 4, depth_z)
        gradient = from_lines(
            gradient_home(
                lax.all_to_all(to_lines(pres), "tx", split_axis=2, concat_axis=1, tiled=True)
            )
        )
        velx_state = velx_state - TIME_STEP * buoyancy * gradient
        diverge = from_lines(
            divergence_home(
                lax.all_to_all(to_lines(velx_state), "tx", split_axis=2, concat_axis=1, tiled=True)
            )
        )
        diverge = diverge + backward_diff(pad_axis(vely, 2), 2, 4, depth_y)
        diverge = diverge + backward_diff(pad_axis(velz, 3), 3, 4, depth_z)
        pres = pres - TIME_STEP * kappa * diverge
        injected = lax.dynamic_index_in_dim(sources, step, 0, keepdims=False)
        pres = jnp.stack([pres[0], pres[1] + injected])
        image = image + pres[0] * pres[1]
        return (pres, velx_state, vely, velz, image)

    pres, velx_state, vely, velz, image = lax.fori_loop(
        0, samples_count, advance, (pres, velx_state, vely, velz, zeros)
    )
    return (image, pres[1])


ROWS = 8
HALO = 7
EXT = ROWS + 2 * HALO
VEXT = ROWS + 7


def block_of(tile):
    zed, rest = tile // 4, tile % 4
    return zed * 4 + ((rest // 2 + zed) % 2) * 2 + rest % 2


def line_matrix(count, forward):
    table = np.zeros((count, count), np.float64)
    for i in range(count):
        for order in range(1, 5):
            plus, minus = (i + order, i - order + 1) if forward else (i + order - 1, i - order)
            if 0 <= plus < count:
                table[plus, i] += COEFS[order - 1]
            if 0 <= minus < count:
                table[minus, i] -= COEFS[order - 1]
    return table


def spectral_matrix(count, offset):
    shift = np.arange(count)[None, :] - np.arange(count)[:, None] + offset
    sign = np.where(shift % 2 == 1, 1.0, -1.0)
    return sign * (4.0 / math.pi) / (2.0 * shift - 1.0) ** 2


def halves(values):
    high = values.astype(jnp.bfloat16)
    return high, (values - high.astype(jnp.float32)).astype(jnp.bfloat16)


def scatter_kernel(tile_ref, load_ref, dense_ref):
    steps = dense_ref.shape[0]
    depth_z = dense_ref.shape[3]
    width = load_ref.shape[2]
    depth_y = ROWS * lax.axis_size("tx")
    start = ROWS * block_of(lax.axis_index("tx"))
    dense_ref[...] = jnp.zeros_like(dense_ref)
    row_ids = lax.broadcasted_iota(jnp.int32, (2 * ROWS, width), 0)
    depth_ids = lax.broadcasted_iota(jnp.int32, (depth_z, width), 0)
    group = 4

    def body(trip, carry):
        for inner in range(group):
            panel = trip * group + inner
            load = load_ref[panel]
            cell = load[steps : steps + 1].astype(jnp.int32)
            zed = cell % depth_z
            line = cell // depth_z
            plane = line // depth_y
            row = line % depth_y - start
            place = jnp.where((row >= 0) & (row < ROWS), plane * ROWS + row, -1)
            mask = jnp.broadcast_to(place, (2 * ROWS, width)) == row_ids
            spot = jnp.where(jnp.broadcast_to(zed, (depth_z, width)) == depth_ids, 1.0, 0.0)
            spot = spot.astype(jnp.bfloat16)
            high, low = halves(load[:steps])
            parts = []
            for part in (high, low):
                part = part.astype(jnp.float32)
                pieces = [
                    jnp.where(mask, jnp.broadcast_to(part[s : s + 1], mask.shape), 0.0)
                    for s in range(steps)
                ]
                parts.append(jnp.concatenate(pieces, axis=0).astype(jnp.bfloat16))
            sums = lax.dot_general(
                jnp.concatenate(parts, axis=1),
                jnp.concatenate([spot, spot], axis=1),
                (((1,), (1,)), ((), ())),
                preferred_element_type=jnp.float32,
            )
            first = tile_ref[panel] * 2
            dense_ref[:, pl.ds(first, 2)] += sums.reshape(steps, 2, ROWS, depth_z)
        return carry

    lax.fori_loop(0, load_ref.shape[0] // group, body, 0)


def wave_kernel(
    fields_ref, dense_ref, xf_ref, xb_ref, zf_ref, zb_ref, out_ref,
    land, pres, velx, vely, velz, buoy, kap, part, image, outx,
    in_send, in_recv, halo_send, halo_recv, out_send, out_recv,
):
    tiles = lax.axis_size("tx")
    me = lax.axis_index("tx")
    block = block_of(me)
    steps = dense_ref.shape[0]
    extent = land.shape[1] // ROWS
    depth_z = land.shape[2]
    octets = extent // 8
    last = tiles - 1
    before = block_of(lax.rem(block + tiles - 1, tiles))
    after = block_of(lax.rem(block + 1, tiles))

    barrier = pltpu.get_barrier_semaphore()

    def greet(k, carry):
        pl.semaphore_signal(
            barrier, inc=1, device_id={"tx": lax.rem(me + k, tiles)},
            device_id_type=pl.DeviceIdType.MESH,
        )
        return carry

    lax.fori_loop(1, tiles, greet, 0)
    pl.semaphore_wait(barrier, tiles - 1)

    def spread(k, plane):
        there = lax.rem(me + k, tiles)
        return pltpu.make_async_remote_copy(
            src_ref=fields_ref.at[:, plane, pl.ds(pl.multiple_of(block_of(there) * ROWS, ROWS), ROWS)],
            dst_ref=land.at[:, pl.ds(pl.multiple_of((me * 2 + plane) * ROWS, ROWS), ROWS)],
            send_sem=in_send.at[plane, k],
            recv_sem=in_recv.at[plane, k],
            device_id={"tx": there},
            device_id_type=pl.DeviceIdType.MESH,
        )

    def spread_start(k, carry):
        for plane in range(2):
            spread(k, plane).start()
        return carry

    def spread_wait(k, carry):
        for plane in range(2):
            spread(k, plane).wait()
        return carry

    lax.fori_loop(1, tiles, spread_start, 0)
    for plane in range(2):
        land[:, pl.ds(pl.multiple_of((me * 2 + plane) * ROWS, ROWS), ROWS)] = fields_ref[
            :, plane, pl.ds(pl.multiple_of(block * ROWS, ROWS), ROWS)
        ]
    for ref in (velx, vely, velz):
        ref[1] = jnp.zeros(ref.shape[1:], jnp.float32)
    image[...] = jnp.zeros_like(image)
    pres[0, 1, HALO : HALO + ROWS] = jnp.zeros((ROWS, extent, depth_z), jnp.float32)
    lax.fori_loop(1, tiles, spread_wait, 0)

    for y in range(ROWS):
        lines = pl.ds(y, extent, stride=ROWS)
        kap[y] = TIME_STEP * land[0, lines, :]
        buoy[4 + y] = TIME_STEP * land[1, lines, :]
        pres[0, 0, HALO + y] = land[2, lines, :]
        velx[0, y] = land[3, lines, :]
        vely[0, 4 + y] = land[4, lines, :]
        velz[0, y] = land[5, lines, :]

    def to_before(ref, low, high, slot):
        return pltpu.make_async_remote_copy(
            src_ref=low, dst_ref=high, send_sem=halo_send.at[0, slot],
            recv_sem=halo_recv.at[0, slot], device_id={"tx": before},
            device_id_type=pl.DeviceIdType.MESH,
        )

    def to_after(ref, high, low, slot):
        return pltpu.make_async_remote_copy(
            src_ref=high, dst_ref=low, send_sem=halo_send.at[1, slot],
            recv_sem=halo_recv.at[1, slot], device_id={"tx": after},
            device_id_type=pl.DeviceIdType.MESH,
        )

    def pres_before(t):
        return to_before(pres, pres.at[t, :, HALO : 2 * HALO], pres.at[t, :, HALO + ROWS : EXT], t)

    def pres_after(t):
        return to_after(pres, pres.at[t, :, ROWS : ROWS + HALO], pres.at[t, :, 0:HALO], t)

    vel_before = to_before(vely, vely.at[0, 4:7], vely.at[0, 12:15], steps)
    vel_after = to_after(vely, vely.at[0, 8:12], vely.at[0, 0:4], steps)
    buoy_before = to_before(buoy, buoy.at[4:7], buoy.at[12:15], steps + 1)
    buoy_after = to_after(buoy, buoy.at[8:12], buoy.at[0:4], steps + 1)

    @pl.when(block > 0)
    def _():
        pres_before(0).start()
        vel_before.start()
        buoy_before.start()

    @pl.when(block < last)
    def _():
        pres_after(0).start()
        vel_after.start()
        buoy_after.start()

    @pl.when(block == 0)
    def _():
        vely[0, 0:4] = jnp.zeros((4, extent, depth_z), jnp.float32)
        buoy[0:4] = jnp.zeros((4, extent, depth_z), jnp.float32)

    @pl.when(block == last)
    def _():
        vely[0, 12:15] = jnp.zeros((3, extent, depth_z), jnp.float32)
        buoy[12:15] = jnp.zeros((3, extent, depth_z), jnp.float32)

    def split(values):
        return halves(values)

    def along_x(table, high, low):
        high = jnp.concatenate([high[y] for y in range(ROWS)], axis=1)
        low = jnp.concatenate([low[y] for y in range(ROWS)], axis=1)
        out = jnp.dot(
            table, jnp.concatenate([high, low, high], axis=0), preferred_element_type=jnp.float32
        )
        return [out[:, y * depth_z : (y + 1) * depth_z] for y in range(ROWS)]

    def along_z(table, high, low):
        high = high.reshape(ROWS * extent, depth_z)
        low = low.reshape(ROWS * extent, depth_z)
        out = jnp.dot(
            jnp.concatenate([high, low, high], axis=1), table, preferred_element_type=jnp.float32
        )
        return out.reshape(ROWS, extent, depth_z)

    def step(t, carry):
        @pl.when(t > 0)
        def _():
            @pl.when(block > 0)
            def _():
                pres_before(t).start()

            @pl.when(block < last)
            def _():
                pres_after(t).start()

        @pl.when(block == 0)
        def _():
            pres[t, :, 0:HALO] = jnp.zeros((2, HALO, extent, depth_z), jnp.float32)

        @pl.when(block == last)
        def _():
            pres[t, :, HALO + ROWS : EXT] = jnp.zeros((2, HALO, extent, depth_z), jnp.float32)

        for w in range(2):
            high, low = split(pres[t, w, HALO : HALO + ROWS])
            own = buoy[4 : 4 + ROWS]
            gradient = along_x(xf_ref[...], high, low)
            for y in range(ROWS):
                velx[w, y] -= buoy[4 + y] * gradient[y]
            velz[w] -= own * along_z(zf_ref[...], high, low)
            high, low = split(velz[w])
            part[w] = along_z(zb_ref[...], high, low)
            high, low = split(velx[w])
            diverge = along_x(xb_ref[...], high, low)
            for y in range(ROWS):
                part[w, y] += diverge[y]

        @pl.when(t == 0)
        def _():
            @pl.when(block > 0)
            def _():
                vel_before.wait_send()
                vel_after.wait_recv()
                buoy_after.wait_recv()

            @pl.when(block < last)
            def _():
                vel_after.wait_send()
                vel_before.wait_recv()
                buoy_before.wait_recv()

        @pl.when(block > 0)
        def _():
            pres_after(t).wait_recv()

        @pl.when(block < last)
        def _():
            pres_before(t).wait_recv()

        for octet in range(octets):
            xs = slice(8 * octet, 8 * octet + 8)
            made = []
            for w in range(2):
                p = pres[t, w, :, xs]
                d = (
                    COEFS[0] * (p[4:19] - p[3:18])
                    + COEFS[1] * (p[5:20] - p[2:17])
                    + COEFS[2] * (p[6:21] - p[1:16])
                    + COEFS[3] * (p[7:22] - p[0:15])
                )
                v = vely[w, :, xs] - buoy[:, xs] * d
                vely[w, :, xs] = v
                d = (
                    COEFS[0] * (v[4:12] - v[3:11])
                    + COEFS[1] * (v[5:13] - v[2:10])
                    + COEFS[2] * (v[6:14] - v[1:9])
                    + COEFS[3] * (v[7:15] - v[0:8])
                )
                new = p[HALO : HALO + ROWS] - kap[:, xs] * (part[w, :, xs] + d)
                if w == 1:
                    new = new + jnp.stack(
                        [
                            dense_ref[t, pl.ds(64 * octet + y, 8, stride=ROWS), :]
                            for y in range(ROWS)
                        ]
                    )
                pres[t + 1, w, HALO : HALO + ROWS, xs] = new
                made.append(new)
            image[:, xs] += made[0] * made[1]
        return carry

    lax.fori_loop(0, steps, step, 0)

    for y in range(ROWS):
        lines = pl.ds(y, extent, stride=ROWS)
        outx[0, lines, :] = image[y]
        outx[1, lines, :] = pres[steps, 1, HALO + y]

    def gather(k, plane):
        there = lax.rem(me + k, tiles)
        return pltpu.make_async_remote_copy(
            src_ref=outx.at[:, pl.ds(pl.multiple_of((there * 2 + plane) * ROWS, ROWS), ROWS)],
            dst_ref=out_ref.at[:, plane, pl.ds(pl.multiple_of(block * ROWS, ROWS), ROWS)],
            send_sem=out_send.at[plane, k],
            recv_sem=out_recv.at[plane, k],
            device_id={"tx": there},
            device_id_type=pl.DeviceIdType.MESH,
        )

    def gather_start(k, carry):
        for plane in range(2):
            gather(k, plane).start()
        return carry

    def gather_wait(k, carry):
        for plane in range(2):
            gather(k, plane).wait()
        return carry

    lax.fori_loop(1, tiles, gather_start, 0)
    for plane in range(2):
        out_ref[:, plane, pl.ds(pl.multiple_of(block * ROWS, ROWS), ROWS)] = outx[
            :, pl.ds(pl.multiple_of((me * 2 + plane) * ROWS, ROWS), ROWS)
        ]

    def sent(t, carry):
        @pl.when(block > 0)
        def _():
            pres_before(t).wait_send()

        @pl.when(block < last)
        def _():
            pres_after(t).wait_send()

        return carry

    lax.fori_loop(0, steps, sent, 0)

    @pl.when(block > 0)
    def _():
        buoy_before.wait_send()

    @pl.when(block < last)
    def _():
        buoy_after.wait_send()

    lax.fori_loop(1, tiles, gather_wait, 0)


def stacked(table, axis):
    high = table.astype(jnp.bfloat16)
    low = (table - high.astype(np.float64)).astype(jnp.bfloat16)
    return jnp.asarray(np.concatenate([high, high, low], axis=axis))


def block_path(kappa, buoyancy, source_state, traces, panel_tile, rcv_index):
    count, depth_y, depth_z = kappa.shape
    tiles = lax.axis_size("tx")
    extent = count * tiles
    panels, steps, width = traces.shape
    load = jnp.concatenate(
        [
            TIME_STEP * traces,
            rcv_index.astype(jnp.float32)[:, None, :],
            jnp.broadcast_to(panel_tile.astype(jnp.float32)[:, :, None], (panels, 1, width)),
        ],
        axis=1,
    )
    load = lax.all_gather(load, "tx", axis=0, tiled=True)
    named = load[:, steps + 1, 0].astype(jnp.int32)
    vmem = pl.BlockSpec(memory_space=pltpu.VMEM)
    dense = pl.pallas_call(
        scatter_kernel,
        out_shape=jax.ShapeDtypeStruct((steps, extent, ROWS, depth_z), jnp.float32),
        in_specs=[pl.BlockSpec(memory_space=pltpu.SMEM), vmem],
        out_specs=vmem,
        compiler_params=pltpu.CompilerParams(vmem_limit_bytes=24 * 1024 * 1024),
    )(named, load)
    dense = dense.reshape(steps, extent * ROWS, depth_z)
    fields = jnp.concatenate([kappa[None], buoyancy[None], source_state], axis=0)
    shape = (extent, depth_z)
    out = pl.pallas_call(
        wave_kernel,
        out_shape=jax.ShapeDtypeStruct((2, count, depth_y, depth_z), jnp.float32),
        in_specs=[vmem] * 6,
        out_specs=vmem,
        scratch_shapes=[
            pltpu.VMEM((6, extent * ROWS, depth_z), jnp.float32),
            pltpu.VMEM((steps + 1, 2, EXT) + shape, jnp.float32),
            pltpu.VMEM((2, ROWS) + shape, jnp.float32),
            pltpu.VMEM((2, VEXT) + shape, jnp.float32),
            pltpu.VMEM((2, ROWS) + shape, jnp.float32),
            pltpu.VMEM((VEXT,) + shape, jnp.float32),
            pltpu.VMEM((ROWS,) + shape, jnp.float32),
            pltpu.VMEM((2, ROWS) + shape, jnp.float32),
            pltpu.VMEM((ROWS,) + shape, jnp.float32),
            pltpu.VMEM((2, extent * ROWS, depth_z), jnp.float32),
            pltpu.SemaphoreType.DMA((2, tiles)),
            pltpu.SemaphoreType.DMA((2, tiles)),
            pltpu.SemaphoreType.DMA((2, steps + 2)),
            pltpu.SemaphoreType.DMA((2, steps + 2)),
            pltpu.SemaphoreType.DMA((2, tiles)),
            pltpu.SemaphoreType.DMA((2, tiles)),
        ],
        compiler_params=pltpu.CompilerParams(
            collective_id=0, has_side_effects=True, vmem_limit_bytes=40 * 1024 * 1024
        ),
    )(
        fields,
        dense,
        stacked(spectral_matrix(extent, 0), 1),
        stacked(spectral_matrix(extent, 1), 1),
        stacked(line_matrix(depth_z, True), 0),
        stacked(line_matrix(depth_z, False), 0),
    )
    return (out[0], out[1])


def on_device(kappa, buoyancy, source_state, traces, panel_tile, rcv_index):
    count, depth_y, depth_z = kappa.shape
    tiles = lax.axis_size("tx")
    extent = count * tiles
    fits = depth_y == ROWS * tiles and depth_z == 128 and traces.shape[2] == 128
    fits = fits and count == 2 and tiles % 4 == 0 and extent % 16 == 0
    path = block_path if fits else transposed_path
    return path(kappa, buoyancy, source_state, traces, panel_tile, rcv_index)


def solution(mesh):
    return jax.shard_map(
        on_device,
        mesh=mesh,
        in_specs=(
            P("tx", None, None),
            P("tx", None, None),
            P(None, ("shots", "tx"), None, None),
            P(("shots", "tx"), None, None),
            P(("shots", "tx"), None),
            P(("shots", "tx"), None),
        ),
        out_specs=(P(("shots", "tx"), None, None), P(("shots", "tx"), None, None)),
        check_vma=False,
    )
```

```python
import math

import jax
import jax.numpy as jnp
import numpy as np
from jax import lax
from jax.experimental import pallas as pl
from jax.experimental.pallas import tpu as pltpu
from jax.sharding import PartitionSpec as P

CAP = 2


COEFS = (1225.0 / 1024.0, -245.0 / 3072.0, 49.0 / 5120.0, -5.0 / 7168.0)
TIME_STEP = 0.15


def window(array, start, count, axis):
    return lax.slice_in_dim(array, start, start + count, axis=axis)


def forward_diff(padded, axis, start, count):
    total = jnp.zeros_like(window(padded, start, count, axis))
    for order in range(1, 5):
        total = total + COEFS[order - 1] * (
            window(padded, start + order, count, axis)
            - window(padded, start - order + 1, count, axis)
        )
    return total


def backward_diff(padded, axis, start, count):
    total = jnp.zeros_like(window(padded, start, count, axis))
    for order in range(1, 5):
        total = total + COEFS[order - 1] * (
            window(padded, start + order - 1, count, axis)
            - window(padded, start - order, count, axis)
        )
    return total


def pad_axis(array, axis):
    widths = [(0, 0)] * array.ndim
    widths[axis] = (4, 4)
    return jnp.pad(array, widths)


def spectral_table(count, offset):
    row_ids = jnp.arange(count, dtype=jnp.int32)[:, None]
    col_ids = jnp.arange(count, dtype=jnp.int32)[None, :]
    shift = col_ids - row_ids + offset
    sign = (1 - 2 * ((shift + 1) % 2)).astype(jnp.float32)
    odd = (2 * shift - 1).astype(jnp.float32)
    return sign * (4.0 / math.pi) / (odd * odd)


def along_lines(table, lines):
    return jnp.einsum("ij,wjkc->wikc", table, lines, precision=lax.Precision.HIGHEST)


def transposed_path(kappa, buoyancy, source_state, traces, panel_tile, rcv_index):
    count = kappa.shape[0]
    depth_y = kappa.shape[1]
    depth_z = kappa.shape[2]
    tiles = lax.axis_size("tx")
    columns = depth_y * depth_z // tiles
    extent = count * tiles
    forward_table = spectral_table(extent, 0)
    backward_table = spectral_table(extent, 1)
    panels = traces.shape[0]
    samples_count = traces.shape[1]
    receivers = traces.shape[2]
    dest = panel_tile[:, 0]
    same = dest[:, None] == dest[None, :]
    earlier = jnp.arange(panels)[None, :] < jnp.arange(panels)[:, None]
    rank = jnp.sum((same & earlier).astype(jnp.int32), axis=1)
    target = dest * CAP + rank
    onehot = (target[:, None] == jnp.arange(tiles * CAP)[None, :]).astype(jnp.float32)
    payload = jnp.concatenate([rcv_index.astype(jnp.float32)[:, None, :], traces], axis=1).reshape(
        panels, -1
    )
    packed = lax.dot_general(
        onehot, payload, (((0,), (0,)), ((), ())), precision=lax.Precision.HIGHEST
    )
    packed = packed.reshape(tiles, CAP, (samples_count + 1) * receivers)
    arrived = lax.all_to_all(packed, "tx", split_axis=0, concat_axis=0, tiled=True).reshape(
        tiles * CAP, samples_count + 1, receivers
    )
    local_index = arrived[:, 0, :].astype(jnp.int32).reshape(-1)
    samples = arrived[:, 1:, :]
    sample_rows = TIME_STEP * jnp.transpose(samples, (0, 2, 1)).reshape(-1, samples_count)
    dense = (
        jnp.zeros((count * depth_y * depth_z, samples_count), jnp.float32)
        .at[local_index]
        .add(sample_rows)
    )
    sources = jnp.transpose(dense).reshape(samples_count, count, depth_y, depth_z)

    def to_lines(field):
        return field.reshape(field.shape[0], count, tiles, columns)

    def from_lines(field):
        return field.reshape(field.shape[0], count, depth_y, depth_z)

    def gradient_home(lines):
        return lax.all_to_all(
            along_lines(forward_table, lines), "tx", split_axis=1, concat_axis=2, tiled=True
        )

    def divergence_home(lines):
        return lax.all_to_all(
            along_lines(backward_table, lines), "tx", split_axis=1, concat_axis=2, tiled=True
        )

    zeros = jnp.zeros_like(source_state[0])
    pres = jnp.stack([source_state[0], zeros])
    velx = jnp.stack([source_state[1], zeros])
    vely = jnp.stack([source_state[2], zeros])
    velz = jnp.stack([source_state[3], zeros])
    velx_state = velx

    def advance(step, carry):
        pres, velx_state, vely, velz, image = carry
        vely = vely - TIME_STEP * buoyancy * forward_diff(pad_axis(pres, 2), 2, 4, depth_y)
        velz = velz - TIME_STEP * buoyancy * forward_diff(pad_axis(pres, 3), 3, 4, depth_z)
        gradient = from_lines(
            gradient_home(
                lax.all_to_all(to_lines(pres), "tx", split_axis=2, concat_axis=1, tiled=True)
            )
        )
        velx_state = velx_state - TIME_STEP * buoyancy * gradient
        diverge = from_lines(
            divergence_home(
                lax.all_to_all(to_lines(velx_state), "tx", split_axis=2, concat_axis=1, tiled=True)
            )
        )
        diverge = diverge + backward_diff(pad_axis(vely, 2), 2, 4, depth_y)
        diverge = diverge + backward_diff(pad_axis(velz, 3), 3, 4, depth_z)
        pres = pres - TIME_STEP * kappa * diverge
        injected = lax.dynamic_index_in_dim(sources, step, 0, keepdims=False)
        pres = jnp.stack([pres[0], pres[1] + injected])
        image = image + pres[0] * pres[1]
        return (pres, velx_state, vely, velz, image)

    pres, velx_state, vely, velz, image = lax.fori_loop(
        0, samples_count, advance, (pres, velx_state, vely, velz, zeros)
    )
    return (image, pres[1])


ROWS = 8
HALO = 7
EXT = ROWS + 2 * HALO
VEXT = ROWS + 7


def block_of(tile):
    zed, rest = tile // 4, tile % 4
    return zed * 4 + ((rest // 2 + zed) % 2) * 2 + rest % 2


def line_matrix(count, forward):
    table = np.zeros((count, count), np.float64)
    for i in range(count):
        for order in range(1, 5):
            plus, minus = (i + order, i - order + 1) if forward else (i + order - 1, i - order)
            if 0 <= plus < count:
                table[plus, i] += COEFS[order - 1]
            if 0 <= minus < count:
                table[minus, i] -= COEFS[order - 1]
    return table


def spectral_matrix(count, offset):
    shift = np.arange(count)[None, :] - np.arange(count)[:, None] + offset
    sign = np.where(shift % 2 == 1, 1.0, -1.0)
    return sign * (4.0 / math.pi) / (2.0 * shift - 1.0) ** 2


def halves(values):
    high = values.astype(jnp.bfloat16)
    return high, (values - high.astype(jnp.float32)).astype(jnp.bfloat16)


def scatter_kernel(tile_ref, load_ref, dense_ref):
    steps = dense_ref.shape[0]
    depth_z = dense_ref.shape[3]
    width = load_ref.shape[2]
    depth_y = ROWS * lax.axis_size("tx")
    start = ROWS * block_of(lax.axis_index("tx"))
    dense_ref[...] = jnp.zeros_like(dense_ref)
    row_ids = lax.broadcasted_iota(jnp.int32, (2 * ROWS, width), 0)
    depth_ids = lax.broadcasted_iota(jnp.int32, (depth_z, width), 0)
    group = 4

    def body(trip, carry):
        for inner in range(group):
            panel = trip * group + inner
            load = load_ref[panel]
            cell = load[steps : steps + 1].astype(jnp.int32)
            zed = cell % depth_z
            line = cell // depth_z
            plane = line // depth_y % 2
            row = line % depth_y - start
            place = jnp.where((row >= 0) & (row < ROWS), plane * ROWS + row, -1)
            mask = jnp.broadcast_to(place, (2 * ROWS, width)) == row_ids
            spot = jnp.where(jnp.broadcast_to(zed, (depth_z, width)) == depth_ids, 1.0, 0.0)
            spot = spot.astype(jnp.bfloat16)
            high, low = halves(load[:steps])
            parts = []
            for part in (high, low):
                part = part.astype(jnp.float32)
                pieces = [
                    jnp.where(mask, jnp.broadcast_to(part[s : s + 1], mask.shape), 0.0)
                    for s in range(steps)
                ]
                parts.append(jnp.concatenate(pieces, axis=0).astype(jnp.bfloat16))
            sums = lax.dot_general(
                jnp.concatenate(parts, axis=1),
                jnp.concatenate([spot, spot], axis=1),
                (((1,), (1,)), ((), ())),
                preferred_element_type=jnp.float32,
            )
            first = tile_ref[panel] * 2
            dense_ref[:, pl.ds(first, 2)] += sums.reshape(steps, 2, ROWS, depth_z)
        return carry

    lax.fori_loop(0, load_ref.shape[0] // group, body, 0)


def meet_all(me, tiles):
    barrier = pltpu.get_barrier_semaphore()

    def greet(k, carry):
        pl.semaphore_signal(
            barrier, inc=1, device_id={"tx": lax.rem(me + k, tiles)},
            device_id_type=pl.DeviceIdType.MESH,
        )
        return carry

    lax.fori_loop(1, tiles, greet, 0)
    pl.semaphore_wait(barrier, tiles - 1)


def spread_kernel(
    kappa_ref, buoyancy_ref, source_ref, traces_ref, tile_ref, index_ref, land, load_ref,
    staged, in_send, in_recv, pass_send, pass_recv,
):
    tiles = lax.axis_size("tx")
    me = lax.axis_index("tx")
    block = block_of(me)
    panels, steps, _ = traces_ref.shape
    cells = 2 * kappa_ref.shape[1] * kappa_ref.shape[2]
    rows = tiles // 4
    row, side, core = me // 4, me % 4 // 2, me % 2

    mine = pl.ds(me * panels, panels)
    load_ref[mine, 0:steps] = TIME_STEP * traces_ref[...]
    cell = (tile_ref[...] * cells + index_ref[...]).astype(jnp.float32)
    load_ref[mine, steps : steps + 1] = cell[:, None, :]
    staged[0] = kappa_ref[...]
    staged[1] = buoyancy_ref[...]
    staged[2:6] = source_ref[...]
    meet_all(me, tiles)

    def at(step_by, side_at, core_at):
        return lax.rem(row + step_by, rows) * 4 + side_at * 2 + core_at

    def pass_on(origin, there, kind, slot):
        block_rows = pl.ds(origin * panels, panels)
        return pltpu.make_async_remote_copy(
            src_ref=load_ref.at[block_rows],
            dst_ref=load_ref.at[block_rows],
            send_sem=pass_send.at[kind, slot],
            recv_sem=pass_recv.at[origin],
            device_id={"tx": there},
            device_id_type=pl.DeviceIdType.MESH,
        )

    across = at(0, 1 - side, core)
    beside = at(0, side, 1 - core)
    along = [pass_on(me, at(j, side, core), 0, j) for j in range(1, rows)]
    over = [pass_on(at(j, side, core), across, 1, j) for j in range(rows)]
    twin = [pass_on(at(j, side, core), beside, 2, j) for j in range(rows)]
    twin += [pass_on(at(j, 1 - side, core), beside, 2, rows + j) for j in range(rows)]
    for copy in along + [over[0], twin[0]]:
        copy.start()

    def spread(k, plane):
        there = lax.rem(me + k, tiles)
        return pltpu.make_async_remote_copy(
            src_ref=staged.at[:, plane, pl.ds(pl.multiple_of(block_of(there) * ROWS, ROWS), ROWS)],
            dst_ref=land.at[:, pl.ds(pl.multiple_of((me * 2 + plane) * ROWS, ROWS), ROWS)],
            send_sem=in_send.at[plane, k],
            recv_sem=in_recv.at[plane, k],
            device_id={"tx": there},
            device_id_type=pl.DeviceIdType.MESH,
        )

    def spread_start(k, carry):
        for plane in range(2):
            spread(k, plane).start()
        return carry

    def spread_wait(k, carry):
        for plane in range(2):
            spread(k, plane).wait()
        return carry

    lax.fori_loop(1, tiles, spread_start, 0)
    for plane in range(2):
        land[:, pl.ds(pl.multiple_of((me * 2 + plane) * ROWS, ROWS), ROWS)] = staged[
            :, plane, pl.ds(pl.multiple_of(block * ROWS, ROWS), ROWS)
        ]
    for j in range(1, rows):
        pass_on(at(j, side, core), across, 0, 0).wait_recv()
        over[j].start()
        twin[j].start()
    for j in range(rows):
        pass_on(at(j, 1 - side, core), across, 0, 0).wait_recv()
        twin[rows + j].start()
    for side_at in range(2):
        for j in range(rows):
            pass_on(at(j, side_at, 1 - core), across, 0, 0).wait_recv()
    lax.fori_loop(1, tiles, spread_wait, 0)
    for copy in along + over + twin:
        copy.wait_send()


def wave_kernel(
    land, dense_ref, xf_ref, xb_ref, zf_ref, zb_ref, out_ref,
    pres, velx, vely, velz, buoy, kap, part, image, outx,
    halo_send, halo_recv, out_send, out_recv,
):
    tiles = lax.axis_size("tx")
    me = lax.axis_index("tx")
    block = block_of(me)
    steps = dense_ref.shape[0]
    extent = land.shape[1] // ROWS
    depth_z = land.shape[2]
    octets = extent // 8
    last = tiles - 1
    before = block_of(lax.rem(block + tiles - 1, tiles))
    after = block_of(lax.rem(block + 1, tiles))

    meet_all(me, tiles)

    for ref in (velx, vely, velz):
        ref[1] = jnp.zeros(ref.shape[1:], jnp.float32)
    image[...] = jnp.zeros_like(image)
    pres[0, 1, HALO : HALO + ROWS] = jnp.zeros((ROWS, extent, depth_z), jnp.float32)

    for y in range(ROWS):
        lines = pl.ds(y, extent, stride=ROWS)
        kap[y] = TIME_STEP * land[0, lines, :]
        buoy[4 + y] = TIME_STEP * land[1, lines, :]
        pres[0, 0, HALO + y] = land[2, lines, :]
        velx[0, y] = land[3, lines, :]
        vely[0, 4 + y] = land[4, lines, :]
        velz[0, y] = land[5, lines, :]

    def to_before(ref, low, high, slot):
        return pltpu.make_async_remote_copy(
            src_ref=low, dst_ref=high, send_sem=halo_send.at[0, slot],
            recv_sem=halo_recv.at[0, slot], device_id={"tx": before},
            device_id_type=pl.DeviceIdType.MESH,
        )

    def to_after(ref, high, low, slot):
        return pltpu.make_async_remote_copy(
            src_ref=high, dst_ref=low, send_sem=halo_send.at[1, slot],
            recv_sem=halo_recv.at[1, slot], device_id={"tx": after},
            device_id_type=pl.DeviceIdType.MESH,
        )

    def pres_before(t, w):
        return to_before(
            pres, pres.at[t, w, HALO : 2 * HALO], pres.at[t, w, HALO + ROWS : EXT], 2 * t + w
        )

    def pres_after(t, w):
        return to_after(pres, pres.at[t, w, ROWS : ROWS + HALO], pres.at[t, w, 0:HALO], 2 * t + w)

    vel_before = to_before(vely, vely.at[0, 4:7], vely.at[0, 12:15], 2 * steps)
    vel_after = to_after(vely, vely.at[0, 8:12], vely.at[0, 0:4], 2 * steps)
    buoy_before = to_before(buoy, buoy.at[4:7], buoy.at[12:15], 2 * steps + 1)
    buoy_after = to_after(buoy, buoy.at[8:12], buoy.at[0:4], 2 * steps + 1)

    @pl.when(block > 0)
    def _():
        pres_before(0, 0).start()
        pres_before(0, 1).start()
        vel_before.start()
        buoy_before.start()

    @pl.when(block < last)
    def _():
        pres_after(0, 0).start()
        pres_after(0, 1).start()
        vel_after.start()
        buoy_after.start()

    @pl.when(block == 0)
    def _():
        vely[0, 0:4] = jnp.zeros((4, extent, depth_z), jnp.float32)
        buoy[0:4] = jnp.zeros((4, extent, depth_z), jnp.float32)

    @pl.when(block == last)
    def _():
        vely[0, 12:15] = jnp.zeros((3, extent, depth_z), jnp.float32)
        buoy[12:15] = jnp.zeros((3, extent, depth_z), jnp.float32)

    def split(values):
        return halves(values)

    def along_x(table, high, low):
        high = jnp.concatenate([high[y] for y in range(ROWS)], axis=1)
        low = jnp.concatenate([low[y] for y in range(ROWS)], axis=1)
        out = jnp.dot(
            table, jnp.concatenate([high, low, high], axis=0), preferred_element_type=jnp.float32
        )
        return [out[:, y * depth_z : (y + 1) * depth_z] for y in range(ROWS)]

    def along_z(table, high, low):
        high = high.reshape(ROWS * extent, depth_z)
        low = low.reshape(ROWS * extent, depth_z)
        out = jnp.dot(
            jnp.concatenate([high, low, high], axis=1), table, preferred_element_type=jnp.float32
        )
        return out.reshape(ROWS, extent, depth_z)

    def step(t, carry):
        @pl.when(block == 0)
        def _():
            pres[t, :, 0:HALO] = jnp.zeros((2, HALO, extent, depth_z), jnp.float32)

        @pl.when(block == last)
        def _():
            pres[t, :, HALO + ROWS : EXT] = jnp.zeros((2, HALO, extent, depth_z), jnp.float32)

        for w in range(2):
            high, low = split(pres[t, w, HALO : HALO + ROWS])
            own = buoy[4 : 4 + ROWS]
            gradient = along_x(xf_ref[...], high, low)
            for y in range(ROWS):
                velx[w, y] -= buoy[4 + y] * gradient[y]
            velz[w] -= own * along_z(zf_ref[...], high, low)
            high, low = split(velz[w])
            part[w] = along_z(zb_ref[...], high, low)
            high, low = split(velx[w])
            diverge = along_x(xb_ref[...], high, low)
            for y in range(ROWS):
                part[w, y] += diverge[y]

        @pl.when(t == 0)
        def _():
            @pl.when(block > 0)
            def _():
                vel_before.wait_send()
                vel_after.wait_recv()
                buoy_after.wait_recv()

            @pl.when(block < last)
            def _():
                vel_after.wait_send()
                vel_before.wait_recv()
                buoy_before.wait_recv()

        for w in range(2):
            @pl.when(block > 0)
            def _():
                pres_after(t, w).wait_recv()

            @pl.when(block < last)
            def _():
                pres_before(t, w).wait_recv()

            for octet in range(octets):
                xs = slice(8 * octet, 8 * octet + 8)
                p = pres[t, w, :, xs]
                d = (
                    COEFS[0] * (p[4:19] - p[3:18])
                    + COEFS[1] * (p[5:20] - p[2:17])
                    + COEFS[2] * (p[6:21] - p[1:16])
                    + COEFS[3] * (p[7:22] - p[0:15])
                )
                v = vely[w, :, xs] - buoy[:, xs] * d
                vely[w, :, xs] = v
                d = (
                    COEFS[0] * (v[4:12] - v[3:11])
                    + COEFS[1] * (v[5:13] - v[2:10])
                    + COEFS[2] * (v[6:14] - v[1:9])
                    + COEFS[3] * (v[7:15] - v[0:8])
                )
                new = p[HALO : HALO + ROWS] - kap[:, xs] * (part[w, :, xs] + d)
                if w == 1:
                    new = new + jnp.stack(
                        [
                            dense_ref[t, pl.ds(64 * octet + y, 8, stride=ROWS), :]
                            for y in range(ROWS)
                        ]
                    )
                pres[t + 1, w, HALO : HALO + ROWS, xs] = new

            @pl.when((block > 0) & (t < steps - 1))
            def _():
                pres_before(t + 1, w).start()

            @pl.when((block < last) & (t < steps - 1))
            def _():
                pres_after(t + 1, w).start()

        own_rows = slice(HALO, HALO + ROWS)
        image[...] += pres[t + 1, 0, own_rows] * pres[t + 1, 1, own_rows]
        return carry

    lax.fori_loop(0, steps, step, 0)

    for y in range(ROWS):
        lines = pl.ds(y, extent, stride=ROWS)
        outx[0, lines, :] = image[y]
        outx[1, lines, :] = pres[steps, 1, HALO + y]

    def gather(k, plane):
        there = lax.rem(me + k, tiles)
        return pltpu.make_async_remote_copy(
            src_ref=outx.at[:, pl.ds(pl.multiple_of((there * 2 + plane) * ROWS, ROWS), ROWS)],
            dst_ref=out_ref.at[:, plane, pl.ds(pl.multiple_of(block * ROWS, ROWS), ROWS)],
            send_sem=out_send.at[plane, k],
            recv_sem=out_recv.at[plane, k],
            device_id={"tx": there},
            device_id_type=pl.DeviceIdType.MESH,
        )

    def gather_start(k, carry):
        for plane in range(2):
            gather(k, plane).start()
        return carry

    def gather_wait(k, carry):
        for plane in range(2):
            gather(k, plane).wait()
        return carry

    lax.fori_loop(1, tiles, gather_start, 0)
    for plane in range(2):
        out_ref[:, plane, pl.ds(pl.multiple_of(block * ROWS, ROWS), ROWS)] = outx[
            :, pl.ds(pl.multiple_of((me * 2 + plane) * ROWS, ROWS), ROWS)
        ]

    def sent(t, carry):
        @pl.when(block > 0)
        def _():
            pres_before(t, 0).wait_send()
            pres_before(t, 1).wait_send()

        @pl.when(block < last)
        def _():
            pres_after(t, 0).wait_send()
            pres_after(t, 1).wait_send()

        return carry

    lax.fori_loop(0, steps, sent, 0)

    @pl.when(block > 0)
    def _():
        buoy_before.wait_send()

    @pl.when(block < last)
    def _():
        buoy_after.wait_send()

    lax.fori_loop(1, tiles, gather_wait, 0)


def stacked(table, axis):
    high = table.astype(jnp.bfloat16)
    low = (table - high.astype(np.float64)).astype(jnp.bfloat16)
    return jnp.asarray(np.concatenate([high, high, low], axis=axis))


def block_path(kappa, buoyancy, source_state, traces, panel_tile, rcv_index):
    count, depth_y, depth_z = kappa.shape
    tiles = lax.axis_size("tx")
    extent = count * tiles
    panels, steps, width = traces.shape
    vmem = pl.BlockSpec(memory_space=pltpu.VMEM)
    land, load = pl.pallas_call(
        spread_kernel,
        out_shape=(
            jax.ShapeDtypeStruct((6, extent * ROWS, depth_z), jnp.float32),
            jax.ShapeDtypeStruct((tiles * panels, steps + 1, width), jnp.float32),
        ),
        in_specs=[vmem] * 6,
        out_specs=(vmem, vmem),
        scratch_shapes=[
            pltpu.VMEM((6, count, depth_y, depth_z), jnp.float32),
            pltpu.SemaphoreType.DMA((2, tiles)),
            pltpu.SemaphoreType.DMA((2, tiles)),
            pltpu.SemaphoreType.DMA((3, tiles)),
            pltpu.SemaphoreType.DMA((tiles,)),
        ],
        compiler_params=pltpu.CompilerParams(
            collective_id=1, has_side_effects=True, vmem_limit_bytes=24 * 1024 * 1024
        ),
    )(kappa, buoyancy, source_state, traces, panel_tile, rcv_index)
    named = load[:, steps, 0].astype(jnp.int32) // (count * depth_y * depth_z)
    dense = pl.pallas_call(
        scatter_kernel,
        out_shape=jax.ShapeDtypeStruct((steps, extent, ROWS, depth_z), jnp.float32),
        in_specs=[pl.BlockSpec(memory_space=pltpu.SMEM), vmem],
        out_specs=vmem,
        compiler_params=pltpu.CompilerParams(vmem_limit_bytes=24 * 1024 * 1024),
    )(named, load)
    dense = dense.reshape(steps, extent * ROWS, depth_z)
    shape = (extent, depth_z)
    out = pl.pallas_call(
        wave_kernel,
        out_shape=jax.ShapeDtypeStruct((2, count, depth_y, depth_z), jnp.float32),
        in_specs=[vmem] * 6,
        out_specs=vmem,
        scratch_shapes=[
            pltpu.VMEM((steps + 1, 2, EXT) + shape, jnp.float32),
            pltpu.VMEM((2, ROWS) + shape, jnp.float32),
            pltpu.VMEM((2, VEXT) + shape, jnp.float32),
            pltpu.VMEM((2, ROWS) + shape, jnp.float32),
            pltpu.VMEM((VEXT,) + shape, jnp.float32),
            pltpu.VMEM((ROWS,) + shape, jnp.float32),
            pltpu.VMEM((2, ROWS) + shape, jnp.float32),
            pltpu.VMEM((ROWS,) + shape, jnp.float32),
            pltpu.VMEM((2, extent * ROWS, depth_z), jnp.float32),
            pltpu.SemaphoreType.DMA((2, 2 * steps + 2)),
            pltpu.SemaphoreType.DMA((2, 2 * steps + 2)),
            pltpu.SemaphoreType.DMA((2, tiles)),
            pltpu.SemaphoreType.DMA((2, tiles)),
        ],
        compiler_params=pltpu.CompilerParams(
            collective_id=0, has_side_effects=True, vmem_limit_bytes=40 * 1024 * 1024
        ),
    )(
        land,
        dense,
        stacked(spectral_matrix(extent, 0), 1),
        stacked(spectral_matrix(extent, 1), 1),
        stacked(line_matrix(depth_z, True), 0),
        stacked(line_matrix(depth_z, False), 0),
    )
    return (out[0], out[1])


def on_device(kappa, buoyancy, source_state, traces, panel_tile, rcv_index):
    count, depth_y, depth_z = kappa.shape
    tiles = lax.axis_size("tx")
    extent = count * tiles
    fits = depth_y == ROWS * tiles and depth_z == 128 and traces.shape[2] == 128
    fits = fits and count == 2 and tiles % 4 == 0 and extent % 16 == 0
    fits = fits and extent * depth_y * depth_z <= 1 << 24
    path = block_path if fits else transposed_path
    return path(kappa, buoyancy, source_state, traces, panel_tile, rcv_index)


def solution(mesh):
    return jax.shard_map(
        on_device,
        mesh=mesh,
        in_specs=(
            P("tx", None, None),
            P("tx", None, None),
            P(None, ("shots", "tx"), None, None),
            P(("shots", "tx"), None, None),
            P(("shots", "tx"), None),
            P(("shots", "tx"), None),
        ),
        out_specs=(P(("shots", "tx"), None, None), P(("shots", "tx"), None, None)),
        check_vma=False,
    )
```

```python
import math

import jax
import jax.numpy as jnp
import numpy as np
from jax import lax
from jax.experimental import pallas as pl
from jax.experimental.pallas import tpu as pltpu
from jax.sharding import PartitionSpec as P

CAP = 2


COEFS = (1225.0 / 1024.0, -245.0 / 3072.0, 49.0 / 5120.0, -5.0 / 7168.0)
TIME_STEP = 0.15


def window(array, start, count, axis):
    return lax.slice_in_dim(array, start, start + count, axis=axis)


def forward_diff(padded, axis, start, count):
    total = jnp.zeros_like(window(padded, start, count, axis))
    for order in range(1, 5):
        total = total + COEFS[order - 1] * (
            window(padded, start + order, count, axis)
            - window(padded, start - order + 1, count, axis)
        )
    return total


def backward_diff(padded, axis, start, count):
    total = jnp.zeros_like(window(padded, start, count, axis))
    for order in range(1, 5):
        total = total + COEFS[order - 1] * (
            window(padded, start + order - 1, count, axis)
            - window(padded, start - order, count, axis)
        )
    return total


def pad_axis(array, axis):
    widths = [(0, 0)] * array.ndim
    widths[axis] = (4, 4)
    return jnp.pad(array, widths)


def spectral_table(count, offset):
    row_ids = jnp.arange(count, dtype=jnp.int32)[:, None]
    col_ids = jnp.arange(count, dtype=jnp.int32)[None, :]
    shift = col_ids - row_ids + offset
    sign = (1 - 2 * ((shift + 1) % 2)).astype(jnp.float32)
    odd = (2 * shift - 1).astype(jnp.float32)
    return sign * (4.0 / math.pi) / (odd * odd)


def along_lines(table, lines):
    return jnp.einsum("ij,wjkc->wikc", table, lines, precision=lax.Precision.HIGHEST)


def transposed_path(kappa, buoyancy, source_state, traces, panel_tile, rcv_index):
    count = kappa.shape[0]
    depth_y = kappa.shape[1]
    depth_z = kappa.shape[2]
    tiles = lax.axis_size("tx")
    columns = depth_y * depth_z // tiles
    extent = count * tiles
    forward_table = spectral_table(extent, 0)
    backward_table = spectral_table(extent, 1)
    panels = traces.shape[0]
    samples_count = traces.shape[1]
    receivers = traces.shape[2]
    dest = panel_tile[:, 0]
    same = dest[:, None] == dest[None, :]
    earlier = jnp.arange(panels)[None, :] < jnp.arange(panels)[:, None]
    rank = jnp.sum((same & earlier).astype(jnp.int32), axis=1)
    target = dest * CAP + rank
    onehot = (target[:, None] == jnp.arange(tiles * CAP)[None, :]).astype(jnp.float32)
    payload = jnp.concatenate([rcv_index.astype(jnp.float32)[:, None, :], traces], axis=1).reshape(
        panels, -1
    )
    packed = lax.dot_general(
        onehot, payload, (((0,), (0,)), ((), ())), precision=lax.Precision.HIGHEST
    )
    packed = packed.reshape(tiles, CAP, (samples_count + 1) * receivers)
    arrived = lax.all_to_all(packed, "tx", split_axis=0, concat_axis=0, tiled=True).reshape(
        tiles * CAP, samples_count + 1, receivers
    )
    local_index = arrived[:, 0, :].astype(jnp.int32).reshape(-1)
    samples = arrived[:, 1:, :]
    sample_rows = TIME_STEP * jnp.transpose(samples, (0, 2, 1)).reshape(-1, samples_count)
    dense = (
        jnp.zeros((count * depth_y * depth_z, samples_count), jnp.float32)
        .at[local_index]
        .add(sample_rows)
    )
    sources = jnp.transpose(dense).reshape(samples_count, count, depth_y, depth_z)

    def to_lines(field):
        return field.reshape(field.shape[0], count, tiles, columns)

    def from_lines(field):
        return field.reshape(field.shape[0], count, depth_y, depth_z)

    def gradient_home(lines):
        return lax.all_to_all(
            along_lines(forward_table, lines), "tx", split_axis=1, concat_axis=2, tiled=True
        )

    def divergence_home(lines):
        return lax.all_to_all(
            along_lines(backward_table, lines), "tx", split_axis=1, concat_axis=2, tiled=True
        )

    zeros = jnp.zeros_like(source_state[0])
    pres = jnp.stack([source_state[0], zeros])
    velx = jnp.stack([source_state[1], zeros])
    vely = jnp.stack([source_state[2], zeros])
    velz = jnp.stack([source_state[3], zeros])
    velx_state = velx

    def advance(step, carry):
        pres, velx_state, vely, velz, image = carry
        vely = vely - TIME_STEP * buoyancy * forward_diff(pad_axis(pres, 2), 2, 4, depth_y)
        velz = velz - TIME_STEP * buoyancy * forward_diff(pad_axis(pres, 3), 3, 4, depth_z)
        gradient = from_lines(
            gradient_home(
                lax.all_to_all(to_lines(pres), "tx", split_axis=2, concat_axis=1, tiled=True)
            )
        )
        velx_state = velx_state - TIME_STEP * buoyancy * gradient
        diverge = from_lines(
            divergence_home(
                lax.all_to_all(to_lines(velx_state), "tx", split_axis=2, concat_axis=1, tiled=True)
            )
        )
        diverge = diverge + backward_diff(pad_axis(vely, 2), 2, 4, depth_y)
        diverge = diverge + backward_diff(pad_axis(velz, 3), 3, 4, depth_z)
        pres = pres - TIME_STEP * kappa * diverge
        injected = lax.dynamic_index_in_dim(sources, step, 0, keepdims=False)
        pres = jnp.stack([pres[0], pres[1] + injected])
        image = image + pres[0] * pres[1]
        return (pres, velx_state, vely, velz, image)

    pres, velx_state, vely, velz, image = lax.fori_loop(
        0, samples_count, advance, (pres, velx_state, vely, velz, zeros)
    )
    return (image, pres[1])


ROWS = 8
HALO = 7
EXT = ROWS + 2 * HALO
VEXT = ROWS + 7
GROUP = 32


def block_of(tile):
    zed, rest = tile // 4, tile % 4
    return zed * 4 + ((rest // 2 + zed) % 2) * 2 + rest % 2


def line_matrix(count, forward):
    table = np.zeros((count, count), np.float64)
    for i in range(count):
        for order in range(1, 5):
            plus, minus = (i + order, i - order + 1) if forward else (i + order - 1, i - order)
            if 0 <= plus < count:
                table[plus, i] += COEFS[order - 1]
            if 0 <= minus < count:
                table[minus, i] -= COEFS[order - 1]
    return table


def spectral_matrix(count, offset):
    shift = np.arange(count)[None, :] - np.arange(count)[:, None] + offset
    sign = np.where(shift % 2 == 1, 1.0, -1.0)
    return sign * (4.0 / math.pi) / (2.0 * shift - 1.0) ** 2


def halves(values):
    high = values.astype(jnp.bfloat16)
    return high, (values - high.astype(jnp.float32)).astype(jnp.bfloat16)


def scatter_kernel(load_ref, dense_ref, named_ref, tile_ref, sem):
    steps = dense_ref.shape[0]
    depth_z = dense_ref.shape[3]
    width = load_ref.shape[2]
    depth_y = ROWS * lax.axis_size("tx")
    start = ROWS * block_of(lax.axis_index("tx"))
    chunks = named_ref.shape[0]
    named = load_ref[:, steps, :].astype(jnp.int32) // (2 * depth_y * depth_z)
    named = named.reshape(chunks, width, width)
    diagonal = lax.broadcasted_iota(jnp.int32, named.shape, 1)
    diagonal = diagonal == lax.broadcasted_iota(jnp.int32, named.shape, 2)
    named_ref[...] = jnp.sum(jnp.where(diagonal, named, 0), axis=1)
    copy = pltpu.make_async_copy(named_ref, tile_ref, sem)
    copy.start()
    dense_ref[...] = jnp.zeros_like(dense_ref)
    copy.wait()
    row_ids = lax.broadcasted_iota(jnp.int32, (2 * ROWS, width), 0)
    depth_ids = lax.broadcasted_iota(jnp.int32, (depth_z, width), 0)
    group = GROUP

    def body(trip, carry):
        made = []
        for inner in range(group):
            panel = trip * group + inner
            load = load_ref[panel]
            cell = load[steps : steps + 1].astype(jnp.int32)
            zed = cell % depth_z
            line = cell // depth_z
            plane = line // depth_y % 2
            row = line % depth_y - start
            place = jnp.where((row >= 0) & (row < ROWS), plane * ROWS + row, -1)
            mask = jnp.broadcast_to(place, (2 * ROWS, width)) == row_ids
            spot = jnp.where(jnp.broadcast_to(zed, (depth_z, width)) == depth_ids, 1.0, 0.0)
            spot = spot.astype(jnp.bfloat16)
            high, low = halves(load[:steps])
            parts = []
            for part in (high, low):
                part = part.astype(jnp.float32)
                pieces = [
                    jnp.where(mask, jnp.broadcast_to(part[s : s + 1], mask.shape), 0.0)
                    for s in range(steps)
                ]
                parts.append(jnp.concatenate(pieces, axis=0).astype(jnp.bfloat16))
            sums = lax.dot_general(
                jnp.concatenate(parts, axis=1),
                jnp.concatenate([spot, spot], axis=1),
                (((1,), (1,)), ((), ())),
                preferred_element_type=jnp.float32,
            )
            made.append(sums.reshape(steps, 2, ROWS, depth_z))
        for inner in range(group):
            panel = trip * group + inner
            first = tile_ref[panel // width, panel % width] * 2
            dense_ref[:, pl.ds(first, 2)] += made[inner]
        return carry

    lax.fori_loop(0, load_ref.shape[0] // group, body, 0)


def meet_all(me, tiles):
    barrier = pltpu.get_barrier_semaphore()

    def greet(k, carry):
        pl.semaphore_signal(
            barrier, inc=1, device_id={"tx": lax.rem(me + k, tiles)},
            device_id_type=pl.DeviceIdType.MESH,
        )
        return carry

    lax.fori_loop(1, tiles, greet, 0)
    pl.semaphore_wait(barrier, tiles - 1)


def spread_kernel(
    kappa_ref, buoyancy_ref, source_ref, traces_ref, tile_ref, index_ref, land, load_ref,
    staged, held, local_sem, in_send, in_recv, pass_send, pass_recv,
):
    tiles = lax.axis_size("tx")
    me = lax.axis_index("tx")
    block = block_of(me)
    panels, steps, _ = traces_ref.shape
    cells = 2 * kappa_ref.shape[1] * kappa_ref.shape[2]
    rows = tiles // 4
    row, side, core = me // 4, me % 4 // 2, me % 2

    stage = [
        pltpu.make_async_copy(traces_ref, held, local_sem.at[0]),
        pltpu.make_async_copy(kappa_ref, staged.at[0], local_sem.at[1]),
        pltpu.make_async_copy(buoyancy_ref, staged.at[1], local_sem.at[2]),
        pltpu.make_async_copy(source_ref, staged.at[2:6], local_sem.at[3]),
    ]
    for copy in stage:
        copy.start()
    first = me * panels
    for panel in range(panels):
        cell = tile_ref[panel] * cells + index_ref[panel : panel + 1]
        load_ref[first + panel, steps : steps + 1] = cell.astype(jnp.float32)
    stage[0].wait()
    load_ref[pl.ds(first, panels), 0:steps] = TIME_STEP * held[...]
    meet_all(me, tiles)

    def at(step_by, side_at, core_at):
        return lax.rem(row + step_by, rows) * 4 + side_at * 2 + core_at

    def pass_on(origin, there, kind, slot):
        block_rows = pl.ds(origin * panels, panels)
        return pltpu.make_async_remote_copy(
            src_ref=load_ref.at[block_rows],
            dst_ref=load_ref.at[block_rows],
            send_sem=pass_send.at[kind, slot],
            recv_sem=pass_recv.at[origin],
            device_id={"tx": there},
            device_id_type=pl.DeviceIdType.MESH,
        )

    across = at(0, 1 - side, core)
    beside = at(0, side, 1 - core)
    along = [pass_on(me, at(j, side, core), 0, j) for j in range(1, rows)]
    over = [pass_on(at(j, side, core), across, 1, j) for j in range(rows)]
    twin = [pass_on(at(j, side, core), beside, 2, j) for j in range(rows)]
    twin += [pass_on(at(j, 1 - side, core), beside, 2, rows + j) for j in range(rows)]
    for copy in along + [over[0], twin[0]]:
        copy.start()

    def spread(k, plane):
        there = lax.rem(me + k, tiles)
        return pltpu.make_async_remote_copy(
            src_ref=staged.at[:, plane, pl.ds(pl.multiple_of(block_of(there) * ROWS, ROWS), ROWS)],
            dst_ref=land.at[:, pl.ds(pl.multiple_of((me * 2 + plane) * ROWS, ROWS), ROWS)],
            send_sem=in_send.at[plane, k],
            recv_sem=in_recv.at[plane, k],
            device_id={"tx": there},
            device_id_type=pl.DeviceIdType.MESH,
        )

    def spread_start(k, carry):
        for plane in range(2):
            spread(k, plane).start()
        return carry

    def spread_wait(k, carry):
        for plane in range(2):
            spread(k, plane).wait()
        return carry

    for copy in stage[1:]:
        copy.wait()
    lax.fori_loop(1, tiles, spread_start, 0)
    for plane in range(2):
        land[:, pl.ds(pl.multiple_of((me * 2 + plane) * ROWS, ROWS), ROWS)] = staged[
            :, plane, pl.ds(pl.multiple_of(block * ROWS, ROWS), ROWS)
        ]
    for j in range(1, rows):
        pass_on(at(j, side, core), across, 0, 0).wait_recv()
        over[j].start()
        twin[j].start()
    for j in range(rows):
        pass_on(at(j, 1 - side, core), across, 0, 0).wait_recv()
        twin[rows + j].start()
    for side_at in range(2):
        for j in range(rows):
            pass_on(at(j, side_at, 1 - core), across, 0, 0).wait_recv()
    lax.fori_loop(1, tiles, spread_wait, 0)
    for copy in along + over + twin:
        copy.wait_send()


def wave_kernel(
    land, dense_ref, xf_ref, xb_ref, zf_ref, zb_ref, out_ref,
    pres, velx, vely, velz, buoy, kap, part, image, outx,
    halo_send, halo_recv, out_send, out_recv,
):
    tiles = lax.axis_size("tx")
    me = lax.axis_index("tx")
    block = block_of(me)
    steps = dense_ref.shape[0]
    extent = land.shape[1] // ROWS
    depth_z = land.shape[2]
    octets = extent // 8
    last = tiles - 1
    before = block_of(lax.rem(block + tiles - 1, tiles))
    after = block_of(lax.rem(block + 1, tiles))

    meet_all(me, tiles)

    for ref in (velx, vely, velz):
        ref[1] = jnp.zeros(ref.shape[1:], jnp.float32)
    image[...] = jnp.zeros_like(image)
    pres[0, 1, HALO : HALO + ROWS] = jnp.zeros((ROWS, extent, depth_z), jnp.float32)

    for y in range(ROWS):
        lines = pl.ds(y, extent, stride=ROWS)
        kap[y] = TIME_STEP * land[0, lines, :]
        buoy[4 + y] = TIME_STEP * land[1, lines, :]
        pres[0, 0, HALO + y] = land[2, lines, :]
        velx[0, y] = land[3, lines, :]
        vely[0, 4 + y] = land[4, lines, :]
        velz[0, y] = land[5, lines, :]

    def to_before(ref, low, high, slot):
        return pltpu.make_async_remote_copy(
            src_ref=low, dst_ref=high, send_sem=halo_send.at[0, slot],
            recv_sem=halo_recv.at[0, slot], device_id={"tx": before},
            device_id_type=pl.DeviceIdType.MESH,
        )

    def to_after(ref, high, low, slot):
        return pltpu.make_async_remote_copy(
            src_ref=high, dst_ref=low, send_sem=halo_send.at[1, slot],
            recv_sem=halo_recv.at[1, slot], device_id={"tx": after},
            device_id_type=pl.DeviceIdType.MESH,
        )

    def pres_before(t, w):
        return to_before(
            pres, pres.at[t, w, HALO : 2 * HALO], pres.at[t, w, HALO + ROWS : EXT], 2 * t + w
        )

    def pres_after(t, w):
        return to_after(pres, pres.at[t, w, ROWS : ROWS + HALO], pres.at[t, w, 0:HALO], 2 * t + w)

    vel_before = to_before(vely, vely.at[0, 4:7], vely.at[0, 12:15], 2 * steps)
    vel_after = to_after(vely, vely.at[0, 8:12], vely.at[0, 0:4], 2 * steps)
    buoy_before = to_before(buoy, buoy.at[4:7], buoy.at[12:15], 2 * steps + 1)
    buoy_after = to_after(buoy, buoy.at[8:12], buoy.at[0:4], 2 * steps + 1)

    @pl.when(block > 0)
    def _():
        pres_before(0, 0).start()
        pres_before(0, 1).start()
        vel_before.start()
        buoy_before.start()

    @pl.when(block < last)
    def _():
        pres_after(0, 0).start()
        pres_after(0, 1).start()
        vel_after.start()
        buoy_after.start()

    @pl.when(block == 0)
    def _():
        vely[0, 0:4] = jnp.zeros((4, extent, depth_z), jnp.float32)
        buoy[0:4] = jnp.zeros((4, extent, depth_z), jnp.float32)

    @pl.when(block == last)
    def _():
        vely[0, 12:15] = jnp.zeros((3, extent, depth_z), jnp.float32)
        buoy[12:15] = jnp.zeros((3, extent, depth_z), jnp.float32)

    def split(values):
        return halves(values)

    def along_x(table, high, low):
        high = jnp.concatenate([high[y] for y in range(ROWS)], axis=1)
        low = jnp.concatenate([low[y] for y in range(ROWS)], axis=1)
        out = jnp.dot(
            table, jnp.concatenate([high, low, high], axis=0), preferred_element_type=jnp.float32
        )
        return [out[:, y * depth_z : (y + 1) * depth_z] for y in range(ROWS)]

    def along_z(table, high, low):
        high = high.reshape(ROWS * extent, depth_z)
        low = low.reshape(ROWS * extent, depth_z)
        out = jnp.dot(
            jnp.concatenate([high, low, high], axis=1), table, preferred_element_type=jnp.float32
        )
        return out.reshape(ROWS, extent, depth_z)

    def step(t, carry):
        @pl.when(block == 0)
        def _():
            pres[t, :, 0:HALO] = jnp.zeros((2, HALO, extent, depth_z), jnp.float32)

        @pl.when(block == last)
        def _():
            pres[t, :, HALO + ROWS : EXT] = jnp.zeros((2, HALO, extent, depth_z), jnp.float32)

        for w in range(2):
            high, low = split(pres[t, w, HALO : HALO + ROWS])
            own = buoy[4 : 4 + ROWS]
            gradient = along_x(xf_ref[...], high, low)
            for y in range(ROWS):
                velx[w, y] -= buoy[4 + y] * gradient[y]
            velz[w] -= own * along_z(zf_ref[...], high, low)
            high, low = split(velz[w])
            part[w] = along_z(zb_ref[...], high, low)
            high, low = split(velx[w])
            diverge = along_x(xb_ref[...], high, low)
            for y in range(ROWS):
                part[w, y] += diverge[y]

        @pl.when(t == 0)
        def _():
            @pl.when(block > 0)
            def _():
                vel_before.wait_send()
                vel_after.wait_recv()
                buoy_after.wait_recv()

            @pl.when(block < last)
            def _():
                vel_after.wait_send()
                vel_before.wait_recv()
                buoy_before.wait_recv()

        for w in range(2):
            @pl.when(block > 0)
            def _():
                pres_after(t, w).wait_recv()

            @pl.when(block < last)
            def _():
                pres_before(t, w).wait_recv()

            for octet in range(octets):
                xs = slice(8 * octet, 8 * octet + 8)
                p = pres[t, w, :, xs]
                d = (
                    COEFS[0] * (p[4:19] - p[3:18])
                    + COEFS[1] * (p[5:20] - p[2:17])
                    + COEFS[2] * (p[6:21] - p[1:16])
                    + COEFS[3] * (p[7:22] - p[0:15])
                )
                v = vely[w, :, xs] - buoy[:, xs] * d
                vely[w, :, xs] = v
                d = (
                    COEFS[0] * (v[4:12] - v[3:11])
                    + COEFS[1] * (v[5:13] - v[2:10])
                    + COEFS[2] * (v[6:14] - v[1:9])
                    + COEFS[3] * (v[7:15] - v[0:8])
                )
                new = p[HALO : HALO + ROWS] - kap[:, xs] * (part[w, :, xs] + d)
                if w == 1:
                    new = new + jnp.stack(
                        [
                            dense_ref[t, pl.ds(64 * octet + y, 8, stride=ROWS), :]
                            for y in range(ROWS)
                        ]
                    )
                pres[t + 1, w, HALO : HALO + ROWS, xs] = new

            @pl.when((block > 0) & (t < steps - 1))
            def _():
                pres_before(t + 1, w).start()

            @pl.when((block < last) & (t < steps - 1))
            def _():
                pres_after(t + 1, w).start()

        own_rows = slice(HALO, HALO + ROWS)
        image[...] += pres[t + 1, 0, own_rows] * pres[t + 1, 1, own_rows]
        return carry

    lax.fori_loop(0, steps, step, 0)

    for y in range(ROWS):
        lines = pl.ds(y, extent, stride=ROWS)
        outx[0, lines, :] = image[y]
        outx[1, lines, :] = pres[steps, 1, HALO + y]

    def gather(k, plane):
        there = lax.rem(me + k, tiles)
        return pltpu.make_async_remote_copy(
            src_ref=outx.at[:, pl.ds(pl.multiple_of((there * 2 + plane) * ROWS, ROWS), ROWS)],
            dst_ref=out_ref.at[:, plane, pl.ds(pl.multiple_of(block * ROWS, ROWS), ROWS)],
            send_sem=out_send.at[plane, k],
            recv_sem=out_recv.at[plane, k],
            device_id={"tx": there},
            device_id_type=pl.DeviceIdType.MESH,
        )

    def gather_start(k, carry):
        for plane in range(2):
            gather(k, plane).start()
        return carry

    def gather_wait(k, carry):
        for plane in range(2):
            gather(k, plane).wait()
        return carry

    lax.fori_loop(1, tiles, gather_start, 0)
    for plane in range(2):
        out_ref[:, plane, pl.ds(pl.multiple_of(block * ROWS, ROWS), ROWS)] = outx[
            :, pl.ds(pl.multiple_of((me * 2 + plane) * ROWS, ROWS), ROWS)
        ]

    def sent(t, carry):
        @pl.when(block > 0)
        def _():
            pres_before(t, 0).wait_send()
            pres_before(t, 1).wait_send()

        @pl.when(block < last)
        def _():
            pres_after(t, 0).wait_send()
            pres_after(t, 1).wait_send()

        return carry

    lax.fori_loop(0, steps, sent, 0)

    @pl.when(block > 0)
    def _():
        buoy_before.wait_send()

    @pl.when(block < last)
    def _():
        buoy_after.wait_send()

    lax.fori_loop(1, tiles, gather_wait, 0)


def stacked(table, axis):
    high = table.astype(jnp.bfloat16)
    low = (table - high.astype(np.float64)).astype(jnp.bfloat16)
    return jnp.asarray(np.concatenate([high, high, low], axis=axis))


def block_path(kappa, buoyancy, source_state, traces, panel_tile, rcv_index):
    count, depth_y, depth_z = kappa.shape
    tiles = lax.axis_size("tx")
    extent = count * tiles
    panels, steps, width = traces.shape
    vmem = pl.BlockSpec(memory_space=pltpu.VMEM)
    land, load = pl.pallas_call(
        spread_kernel,
        out_shape=(
            jax.ShapeDtypeStruct((6, extent * ROWS, depth_z), jnp.float32),
            jax.ShapeDtypeStruct((tiles * panels, steps + 1, width), jnp.float32),
        ),
        in_specs=[pl.BlockSpec(memory_space=pltpu.HBM)] * 4
        + [pl.BlockSpec(memory_space=pltpu.SMEM), vmem],
        out_specs=(vmem, vmem),
        scratch_shapes=[
            pltpu.VMEM((6, count, depth_y, depth_z), jnp.float32),
            pltpu.VMEM((panels, steps, width), jnp.float32),
            pltpu.SemaphoreType.DMA((4,)),
            pltpu.SemaphoreType.DMA((2, tiles)),
            pltpu.SemaphoreType.DMA((2, tiles)),
            pltpu.SemaphoreType.DMA((3, tiles)),
            pltpu.SemaphoreType.DMA((tiles,)),
        ],
        compiler_params=pltpu.CompilerParams(
            collective_id=1, has_side_effects=True, vmem_limit_bytes=24 * 1024 * 1024
        ),
    )(kappa, buoyancy, source_state, traces, panel_tile.reshape(-1), rcv_index)
    dense = pl.pallas_call(
        scatter_kernel,
        out_shape=jax.ShapeDtypeStruct((steps, extent, ROWS, depth_z), jnp.float32),
        in_specs=[vmem],
        out_specs=vmem,
        scratch_shapes=[
            pltpu.VMEM((tiles * panels // width, width), jnp.int32),
            pltpu.SMEM((tiles * panels // width, width), jnp.int32),
            pltpu.SemaphoreType.DMA,
        ],
        compiler_params=pltpu.CompilerParams(vmem_limit_bytes=24 * 1024 * 1024),
    )(load)
    dense = dense.reshape(steps, extent * ROWS, depth_z)
    shape = (extent, depth_z)
    out = pl.pallas_call(
        wave_kernel,
        out_shape=jax.ShapeDtypeStruct((2, count, depth_y, depth_z), jnp.float32),
        in_specs=[vmem] * 6,
        out_specs=vmem,
        scratch_shapes=[
            pltpu.VMEM((steps + 1, 2, EXT) + shape, jnp.float32),
            pltpu.VMEM((2, ROWS) + shape, jnp.float32),
            pltpu.VMEM((2, VEXT) + shape, jnp.float32),
            pltpu.VMEM((2, ROWS) + shape, jnp.float32),
            pltpu.VMEM((VEXT,) + shape, jnp.float32),
            pltpu.VMEM((ROWS,) + shape, jnp.float32),
            pltpu.VMEM((2, ROWS) + shape, jnp.float32),
            pltpu.VMEM((ROWS,) + shape, jnp.float32),
            pltpu.VMEM((2, extent * ROWS, depth_z), jnp.float32),
            pltpu.SemaphoreType.DMA((2, 2 * steps + 2)),
            pltpu.SemaphoreType.DMA((2, 2 * steps + 2)),
            pltpu.SemaphoreType.DMA((2, tiles)),
            pltpu.SemaphoreType.DMA((2, tiles)),
        ],
        compiler_params=pltpu.CompilerParams(
            collective_id=0, has_side_effects=True, vmem_limit_bytes=40 * 1024 * 1024
        ),
    )(
        land,
        dense,
        stacked(spectral_matrix(extent, 0), 1),
        stacked(spectral_matrix(extent, 1), 1),
        stacked(line_matrix(depth_z, True), 0),
        stacked(line_matrix(depth_z, False), 0),
    )
    return (out[0], out[1])


def on_device(kappa, buoyancy, source_state, traces, panel_tile, rcv_index):
    count, depth_y, depth_z = kappa.shape
    tiles = lax.axis_size("tx")
    extent = count * tiles
    fits = depth_y == ROWS * tiles and depth_z == 128 and traces.shape[2] == 128
    fits = fits and count == 2 and tiles % 4 == 0 and extent % 16 == 0
    fits = fits and extent * depth_y * depth_z <= 1 << 24
    fits = fits and traces.shape[0] * tiles % 128 == 0
    path = block_path if fits else transposed_path
    return path(kappa, buoyancy, source_state, traces, panel_tile, rcv_index)


def solution(mesh):
    return jax.shard_map(
        on_device,
        mesh=mesh,
        in_specs=(
            P("tx", None, None),
            P("tx", None, None),
            P(None, ("shots", "tx"), None, None),
            P(("shots", "tx"), None, None),
            P(("shots", "tx"), None),
            P(("shots", "tx"), None),
        ),
        out_specs=(P(("shots", "tx"), None, None), P(("shots", "tx"), None, None)),
        check_vma=False,
    )
```

```python
import math

import jax
import jax.numpy as jnp
import numpy as np
from jax import lax
from jax.experimental import pallas as pl
from jax.experimental.pallas import tpu as pltpu
from jax.sharding import PartitionSpec as P

CAP = 2


COEFS = (1225.0 / 1024.0, -245.0 / 3072.0, 49.0 / 5120.0, -5.0 / 7168.0)
TIME_STEP = 0.15


def window(array, start, count, axis):
    return lax.slice_in_dim(array, start, start + count, axis=axis)


def forward_diff(padded, axis, start, count):
    total = jnp.zeros_like(window(padded, start, count, axis))
    for order in range(1, 5):
        total = total + COEFS[order - 1] * (
            window(padded, start + order, count, axis)
            - window(padded, start - order + 1, count, axis)
        )
    return total


def backward_diff(padded, axis, start, count):
    total = jnp.zeros_like(window(padded, start, count, axis))
    for order in range(1, 5):
        total = total + COEFS[order - 1] * (
            window(padded, start + order - 1, count, axis)
            - window(padded, start - order, count, axis)
        )
    return total


def pad_axis(array, axis):
    widths = [(0, 0)] * array.ndim
    widths[axis] = (4, 4)
    return jnp.pad(array, widths)


def spectral_table(count, offset):
    row_ids = jnp.arange(count, dtype=jnp.int32)[:, None]
    col_ids = jnp.arange(count, dtype=jnp.int32)[None, :]
    shift = col_ids - row_ids + offset
    sign = (1 - 2 * ((shift + 1) % 2)).astype(jnp.float32)
    odd = (2 * shift - 1).astype(jnp.float32)
    return sign * (4.0 / math.pi) / (odd * odd)


def along_lines(table, lines):
    return jnp.einsum("ij,wjkc->wikc", table, lines, precision=lax.Precision.HIGHEST)


def transposed_path(kappa, buoyancy, source_state, traces, panel_tile, rcv_index):
    count = kappa.shape[0]
    depth_y = kappa.shape[1]
    depth_z = kappa.shape[2]
    tiles = lax.axis_size("tx")
    columns = depth_y * depth_z // tiles
    extent = count * tiles
    forward_table = spectral_table(extent, 0)
    backward_table = spectral_table(extent, 1)
    panels = traces.shape[0]
    samples_count = traces.shape[1]
    receivers = traces.shape[2]
    dest = panel_tile[:, 0]
    same = dest[:, None] == dest[None, :]
    earlier = jnp.arange(panels)[None, :] < jnp.arange(panels)[:, None]
    rank = jnp.sum((same & earlier).astype(jnp.int32), axis=1)
    target = dest * CAP + rank
    onehot = (target[:, None] == jnp.arange(tiles * CAP)[None, :]).astype(jnp.float32)
    payload = jnp.concatenate([rcv_index.astype(jnp.float32)[:, None, :], traces], axis=1).reshape(
        panels, -1
    )
    packed = lax.dot_general(
        onehot, payload, (((0,), (0,)), ((), ())), precision=lax.Precision.HIGHEST
    )
    packed = packed.reshape(tiles, CAP, (samples_count + 1) * receivers)
    arrived = lax.all_to_all(packed, "tx", split_axis=0, concat_axis=0, tiled=True).reshape(
        tiles * CAP, samples_count + 1, receivers
    )
    local_index = arrived[:, 0, :].astype(jnp.int32).reshape(-1)
    samples = arrived[:, 1:, :]
    sample_rows = TIME_STEP * jnp.transpose(samples, (0, 2, 1)).reshape(-1, samples_count)
    dense = (
        jnp.zeros((count * depth_y * depth_z, samples_count), jnp.float32)
        .at[local_index]
        .add(sample_rows)
    )
    sources = jnp.transpose(dense).reshape(samples_count, count, depth_y, depth_z)

    def to_lines(field):
        return field.reshape(field.shape[0], count, tiles, columns)

    def from_lines(field):
        return field.reshape(field.shape[0], count, depth_y, depth_z)

    def gradient_home(lines):
        return lax.all_to_all(
            along_lines(forward_table, lines), "tx", split_axis=1, concat_axis=2, tiled=True
        )

    def divergence_home(lines):
        return lax.all_to_all(
            along_lines(backward_table, lines), "tx", split_axis=1, concat_axis=2, tiled=True
        )

    zeros = jnp.zeros_like(source_state[0])
    pres = jnp.stack([source_state[0], zeros])
    velx = jnp.stack([source_state[1], zeros])
    vely = jnp.stack([source_state[2], zeros])
    velz = jnp.stack([source_state[3], zeros])
    velx_state = velx

    def advance(step, carry):
        pres, velx_state, vely, velz, image = carry
        vely = vely - TIME_STEP * buoyancy * forward_diff(pad_axis(pres, 2), 2, 4, depth_y)
        velz = velz - TIME_STEP * buoyancy * forward_diff(pad_axis(pres, 3), 3, 4, depth_z)
        gradient = from_lines(
            gradient_home(
                lax.all_to_all(to_lines(pres), "tx", split_axis=2, concat_axis=1, tiled=True)
            )
        )
        velx_state = velx_state - TIME_STEP * buoyancy * gradient
        diverge = from_lines(
            divergence_home(
                lax.all_to_all(to_lines(velx_state), "tx", split_axis=2, concat_axis=1, tiled=True)
            )
        )
        diverge = diverge + backward_diff(pad_axis(vely, 2), 2, 4, depth_y)
        diverge = diverge + backward_diff(pad_axis(velz, 3), 3, 4, depth_z)
        pres = pres - TIME_STEP * kappa * diverge
        injected = lax.dynamic_index_in_dim(sources, step, 0, keepdims=False)
        pres = jnp.stack([pres[0], pres[1] + injected])
        image = image + pres[0] * pres[1]
        return (pres, velx_state, vely, velz, image)

    pres, velx_state, vely, velz, image = lax.fori_loop(
        0, samples_count, advance, (pres, velx_state, vely, velz, zeros)
    )
    return (image, pres[1])


ROWS = 8
HALO = 7
EXT = ROWS + 2 * HALO
VEXT = ROWS + 7
SHARES = 2
GROUP = 32


def block_of(tile):
    zed, rest = tile // 4, tile % 4
    return zed * 4 + ((rest // 2 + zed) % 2) * 2 + rest % 2


def line_matrix(count, forward):
    table = np.zeros((count, count), np.float64)
    for i in range(count):
        for order in range(1, 5):
            plus, minus = (i + order, i - order + 1) if forward else (i + order - 1, i - order)
            if 0 <= plus < count:
                table[plus, i] += COEFS[order - 1]
            if 0 <= minus < count:
                table[minus, i] -= COEFS[order - 1]
    return table


def spectral_matrix(count, offset):
    shift = np.arange(count)[None, :] - np.arange(count)[:, None] + offset
    sign = np.where(shift % 2 == 1, 1.0, -1.0)
    return sign * (4.0 / math.pi) / (2.0 * shift - 1.0) ** 2


def halves(values):
    high = values.astype(jnp.bfloat16)
    return high, (values - high.astype(jnp.float32)).astype(jnp.bfloat16)


def scatter_kernel(load_ref, dense_ref, named_ref, tile_ref, sem):
    steps = dense_ref.shape[0]
    depth_z = dense_ref.shape[3]
    width = load_ref.shape[2]
    depth_y = ROWS * lax.axis_size("tx")
    start = ROWS * block_of(lax.axis_index("tx"))
    chunks = named_ref.shape[0]
    named = load_ref[:, steps, :].astype(jnp.int32) // (2 * depth_y * depth_z)
    named = named.reshape(chunks, width, width)
    diagonal = lax.broadcasted_iota(jnp.int32, named.shape, 1)
    diagonal = diagonal == lax.broadcasted_iota(jnp.int32, named.shape, 2)
    named_ref[...] = jnp.sum(jnp.where(diagonal, named, 0), axis=1)
    copy = pltpu.make_async_copy(named_ref, tile_ref, sem)
    copy.start()
    dense_ref[...] = jnp.zeros_like(dense_ref)
    copy.wait()
    row_ids = lax.broadcasted_iota(jnp.int32, (2 * ROWS, width), 0)
    depth_ids = lax.broadcasted_iota(jnp.int32, (depth_z, width), 0)
    group = GROUP

    def body(trip, carry):
        made = []
        for inner in range(group):
            panel = trip * group + inner
            load = load_ref[panel]
            cell = load[steps : steps + 1].astype(jnp.int32)
            zed = cell % depth_z
            line = cell // depth_z
            plane = line // depth_y % 2
            row = line % depth_y - start
            place = jnp.where((row >= 0) & (row < ROWS), plane * ROWS + row, -1)
            mask = jnp.broadcast_to(place, (2 * ROWS, width)) == row_ids
            spot = jnp.where(jnp.broadcast_to(zed, (depth_z, width)) == depth_ids, 1.0, 0.0)
            spot = spot.astype(jnp.bfloat16)
            high, low = halves(load[:steps])
            parts = []
            for part in (high, low):
                part = part.astype(jnp.float32)
                pieces = [
                    jnp.where(mask, jnp.broadcast_to(part[s : s + 1], mask.shape), 0.0)
                    for s in range(steps)
                ]
                parts.append(jnp.concatenate(pieces, axis=0).astype(jnp.bfloat16))
            sums = lax.dot_general(
                jnp.concatenate(parts, axis=1),
                jnp.concatenate([spot, spot], axis=1),
                (((1,), (1,)), ((), ())),
                preferred_element_type=jnp.float32,
            )
            made.append(sums.reshape(steps, 2, ROWS, depth_z))
        for inner in range(group):
            panel = trip * group + inner
            first = tile_ref[panel // width, panel % width] * 2
            dense_ref[:, pl.ds(first, 2)] += made[inner]
        return carry

    lax.fori_loop(0, load_ref.shape[0] // group, body, 0)


def meet_all(me, tiles):
    barrier = pltpu.get_barrier_semaphore()

    def greet(k, carry):
        pl.semaphore_signal(
            barrier, inc=1, device_id={"tx": lax.rem(me + k, tiles)},
            device_id_type=pl.DeviceIdType.MESH,
        )
        return carry

    lax.fori_loop(1, tiles, greet, 0)
    pl.semaphore_wait(barrier, tiles - 1)


def spread_kernel(
    kappa_ref, buoyancy_ref, source_ref, traces_ref, tile_ref, index_ref, land, load_ref,
    staged, held, local_sem, in_send, in_recv, pass_send, pass_recv,
):
    tiles = lax.axis_size("tx")
    me = lax.axis_index("tx")
    block = block_of(me)
    panels, steps, _ = traces_ref.shape
    cells = 2 * kappa_ref.shape[1] * kappa_ref.shape[2]
    rows = tiles // 4
    row, side, core = me // 4, me % 4 // 2, me % 2

    stage = [
        pltpu.make_async_copy(traces_ref, held, local_sem.at[0]),
        pltpu.make_async_copy(kappa_ref, staged.at[0], local_sem.at[1]),
        pltpu.make_async_copy(buoyancy_ref, staged.at[1], local_sem.at[2]),
        pltpu.make_async_copy(source_ref, staged.at[2:6], local_sem.at[3]),
    ]
    for copy in stage:
        copy.start()
    first = me * panels
    for panel in range(panels):
        cell = tile_ref[panel] * cells + index_ref[panel : panel + 1]
        load_ref[first + panel, steps : steps + 1] = cell.astype(jnp.float32)
    stage[0].wait()
    load_ref[pl.ds(first, panels), 0:steps] = TIME_STEP * held[...]
    meet_all(me, tiles)

    def at(step_by, side_at, core_at):
        return lax.rem(row + step_by, rows) * 4 + side_at * 2 + core_at

    share = panels // SHARES

    def pass_on(origin, there, kind, slot, piece):
        block_rows = pl.ds(origin * panels + piece * share, share)
        return pltpu.make_async_remote_copy(
            src_ref=load_ref.at[block_rows],
            dst_ref=load_ref.at[block_rows],
            send_sem=pass_send.at[kind, slot, piece],
            recv_sem=pass_recv.at[origin, piece],
            device_id={"tx": there},
            device_id_type=pl.DeviceIdType.MESH,
        )

    across = at(0, 1 - side, core)
    beside = at(0, side, 1 - core)
    pieces = range(SHARES)
    along = [[pass_on(me, at(j, side, core), 0, j, i) for i in pieces] for j in range(1, rows)]
    over = [[pass_on(at(j, side, core), across, 1, j, i) for i in pieces] for j in range(rows)]
    twin = [[pass_on(at(j, side, core), beside, 2, j, i) for i in pieces] for j in range(rows)]
    twin += [
        [pass_on(at(j, 1 - side, core), beside, 2, rows + j, i) for i in pieces]
        for j in range(rows)
    ]
    for i in pieces:
        for copies in along + [over[0], twin[0]]:
            copies[i].start()

    def spread(k, plane):
        there = lax.rem(me + k, tiles)
        return pltpu.make_async_remote_copy(
            src_ref=staged.at[:, plane, pl.ds(pl.multiple_of(block_of(there) * ROWS, ROWS), ROWS)],
            dst_ref=land.at[:, pl.ds(pl.multiple_of((me * 2 + plane) * ROWS, ROWS), ROWS)],
            send_sem=in_send.at[plane, k],
            recv_sem=in_recv.at[plane, k],
            device_id={"tx": there},
            device_id_type=pl.DeviceIdType.MESH,
        )

    def spread_start(k, carry):
        for plane in range(2):
            spread(k, plane).start()
        return carry

    def spread_wait(k, carry):
        for plane in range(2):
            spread(k, plane).wait()
        return carry

    for copy in stage[1:]:
        copy.wait()
    lax.fori_loop(1, tiles, spread_start, 0)
    for plane in range(2):
        land[:, pl.ds(pl.multiple_of((me * 2 + plane) * ROWS, ROWS), ROWS)] = staged[
            :, plane, pl.ds(pl.multiple_of(block * ROWS, ROWS), ROWS)
        ]
    for i in pieces:
        for j in range(1, rows):
            pass_on(at(j, side, core), across, 0, 0, i).wait_recv()
            over[j][i].start()
            twin[j][i].start()
        pass_on(at(0, 1 - side, core), across, 0, 0, i).wait_recv()
        twin[rows][i].start()
    for i in pieces:
        for j in range(1, rows):
            pass_on(at(j, 1 - side, core), across, 0, 0, i).wait_recv()
            twin[rows + j][i].start()
    for i in pieces:
        for side_at in range(2):
            for j in range(rows):
                pass_on(at(j, side_at, 1 - core), across, 0, 0, i).wait_recv()
    lax.fori_loop(1, tiles, spread_wait, 0)
    for copies in along + over + twin:
        for copy in copies:
            copy.wait_send()


def wave_kernel(
    land, dense_ref, xf_ref, xb_ref, zf_ref, zb_ref, out_ref,
    pres, velx, vely, velz, buoy, kap, part, image, outx,
    halo_send, halo_recv, out_send, out_recv,
):
    tiles = lax.axis_size("tx")
    me = lax.axis_index("tx")
    block = block_of(me)
    steps = dense_ref.shape[0]
    extent = land.shape[1] // ROWS
    depth_z = land.shape[2]
    octets = extent // 8
    last = tiles - 1
    before = block_of(lax.rem(block + tiles - 1, tiles))
    after = block_of(lax.rem(block + 1, tiles))

    meet_all(me, tiles)

    for ref in (velx, vely, velz):
        ref[1] = jnp.zeros(ref.shape[1:], jnp.float32)
    image[...] = jnp.zeros_like(image)
    pres[0, 1] = jnp.zeros((EXT, extent, depth_z), jnp.float32)

    for y in range(ROWS):
        lines = pl.ds(y, extent, stride=ROWS)
        kap[y] = TIME_STEP * land[0, lines, :]
        buoy[4 + y] = TIME_STEP * land[1, lines, :]
        pres[0, 0, HALO + y] = land[2, lines, :]
        velx[0, y] = land[3, lines, :]
        vely[0, 4 + y] = land[4, lines, :]
        velz[0, y] = land[5, lines, :]

    def to_before(ref, low, high, slot):
        return pltpu.make_async_remote_copy(
            src_ref=low, dst_ref=high, send_sem=halo_send.at[0, slot],
            recv_sem=halo_recv.at[0, slot], device_id={"tx": before},
            device_id_type=pl.DeviceIdType.MESH,
        )

    def to_after(ref, high, low, slot):
        return pltpu.make_async_remote_copy(
            src_ref=high, dst_ref=low, send_sem=halo_send.at[1, slot],
            recv_sem=halo_recv.at[1, slot], device_id={"tx": after},
            device_id_type=pl.DeviceIdType.MESH,
        )

    def pres_before(t, w):
        return to_before(
            pres, pres.at[t, w, HALO : 2 * HALO], pres.at[t, w, HALO + ROWS : EXT], 2 * t + w
        )

    def pres_after(t, w):
        return to_after(pres, pres.at[t, w, ROWS : ROWS + HALO], pres.at[t, w, 0:HALO], 2 * t + w)

    vel_before = to_before(vely, vely.at[0, 4:7], vely.at[0, 12:15], 2 * steps)
    vel_after = to_after(vely, vely.at[0, 8:12], vely.at[0, 0:4], 2 * steps)
    buoy_before = to_before(buoy, buoy.at[4:7], buoy.at[12:15], 2 * steps + 1)
    buoy_after = to_after(buoy, buoy.at[8:12], buoy.at[0:4], 2 * steps + 1)

    @pl.when(block > 0)
    def _():
        pres_before(0, 0).start()
        vel_before.start()
        buoy_before.start()

    @pl.when(block < last)
    def _():
        pres_after(0, 0).start()
        vel_after.start()
        buoy_after.start()

    @pl.when(block == 0)
    def _():
        vely[0, 0:4] = jnp.zeros((4, extent, depth_z), jnp.float32)
        buoy[0:4] = jnp.zeros((4, extent, depth_z), jnp.float32)

    @pl.when(block == last)
    def _():
        vely[0, 12:15] = jnp.zeros((3, extent, depth_z), jnp.float32)
        buoy[12:15] = jnp.zeros((3, extent, depth_z), jnp.float32)

    def split(values):
        return halves(values)

    def along_x(table, high, low):
        high = jnp.concatenate([high[y] for y in range(ROWS)], axis=1)
        low = jnp.concatenate([low[y] for y in range(ROWS)], axis=1)
        out = jnp.dot(
            table, jnp.concatenate([high, low, high], axis=0), preferred_element_type=jnp.float32
        )
        return [out[:, y * depth_z : (y + 1) * depth_z] for y in range(ROWS)]

    def along_z(table, high, low):
        high = high.reshape(ROWS * extent, depth_z)
        low = low.reshape(ROWS * extent, depth_z)
        out = jnp.dot(
            jnp.concatenate([high, low, high], axis=1), table, preferred_element_type=jnp.float32
        )
        return out.reshape(ROWS, extent, depth_z)

    def local(t, w):
        high, low = split(pres[t, w, HALO : HALO + ROWS])
        gradient = along_x(xf_ref[...], high, low)
        for y in range(ROWS):
            velx[w, y] -= buoy[4 + y] * gradient[y]
        velz[w] -= buoy[4 : 4 + ROWS] * along_z(zf_ref[...], high, low)
        high, low = split(velz[w])
        part[w] = along_z(zb_ref[...], high, low)
        high, low = split(velx[w])
        diverge = along_x(xb_ref[...], high, low)
        for y in range(ROWS):
            part[w, y] += diverge[y]

    for w in range(2):
        local(0, w)

    def step(t, carry):
        @pl.when(block == 0)
        def _():
            pres[t, :, 0:HALO] = jnp.zeros((2, HALO, extent, depth_z), jnp.float32)

        @pl.when(block == last)
        def _():
            pres[t, :, HALO + ROWS : EXT] = jnp.zeros((2, HALO, extent, depth_z), jnp.float32)

        @pl.when(t == 0)
        def _():
            @pl.when(block > 0)
            def _():
                vel_before.wait_send()
                vel_after.wait_recv()
                buoy_after.wait_recv()

            @pl.when(block < last)
            def _():
                vel_after.wait_send()
                vel_before.wait_recv()
                buoy_before.wait_recv()

        for w in range(2):
            @pl.when((block > 0) & (t >= w))
            def _():
                pres_after(t, w).wait_recv()

            @pl.when((block < last) & (t >= w))
            def _():
                pres_before(t, w).wait_recv()

            for octet in range(octets):
                xs = slice(8 * octet, 8 * octet + 8)
                p = pres[t, w, :, xs]
                d = (
                    COEFS[0] * (p[4:19] - p[3:18])
                    + COEFS[1] * (p[5:20] - p[2:17])
                    + COEFS[2] * (p[6:21] - p[1:16])
                    + COEFS[3] * (p[7:22] - p[0:15])
                )
                v = vely[w, :, xs] - buoy[:, xs] * d
                vely[w, :, xs] = v
                d = (
                    COEFS[0] * (v[4:12] - v[3:11])
                    + COEFS[1] * (v[5:13] - v[2:10])
                    + COEFS[2] * (v[6:14] - v[1:9])
                    + COEFS[3] * (v[7:15] - v[0:8])
                )
                new = p[HALO : HALO + ROWS] - kap[:, xs] * (part[w, :, xs] + d)
                if w == 1:
                    new = new + jnp.stack(
                        [
                            dense_ref[t, pl.ds(64 * octet + y, 8, stride=ROWS), :]
                            for y in range(ROWS)
                        ]
                    )
                pres[t + 1, w, HALO : HALO + ROWS, xs] = new

            @pl.when((block > 0) & (t < steps - 1))
            def _():
                pres_before(t + 1, w).start()

            @pl.when((block < last) & (t < steps - 1))
            def _():
                pres_after(t + 1, w).start()

            @pl.when(t < steps - 1)
            def _():
                local(t + 1, w)

        own_rows = slice(HALO, HALO + ROWS)
        image[...] += pres[t + 1, 0, own_rows] * pres[t + 1, 1, own_rows]
        return carry

    lax.fori_loop(0, steps, step, 0)

    for y in range(ROWS):
        lines = pl.ds(y, extent, stride=ROWS)
        outx[0, lines, :] = image[y]
        outx[1, lines, :] = pres[steps, 1, HALO + y]

    def gather(k, plane):
        there = lax.rem(me + k, tiles)
        return pltpu.make_async_remote_copy(
            src_ref=outx.at[:, pl.ds(pl.multiple_of((there * 2 + plane) * ROWS, ROWS), ROWS)],
            dst_ref=out_ref.at[:, plane, pl.ds(pl.multiple_of(block * ROWS, ROWS), ROWS)],
            send_sem=out_send.at[plane, k],
            recv_sem=out_recv.at[plane, k],
            device_id={"tx": there},
            device_id_type=pl.DeviceIdType.MESH,
        )

    def gather_start(k, carry):
        for plane in range(2):
            gather(k, plane).start()
        return carry

    def gather_wait(k, carry):
        for plane in range(2):
            gather(k, plane).wait()
        return carry

    lax.fori_loop(1, tiles, gather_start, 0)
    for plane in range(2):
        out_ref[:, plane, pl.ds(pl.multiple_of(block * ROWS, ROWS), ROWS)] = outx[
            :, pl.ds(pl.multiple_of((me * 2 + plane) * ROWS, ROWS), ROWS)
        ]

    def sent(t, carry):
        @pl.when(block > 0)
        def _():
            pres_before(t, 0).wait_send()

        @pl.when((block > 0) & (t > 0))
        def _():
            pres_before(t, 1).wait_send()

        @pl.when(block < last)
        def _():
            pres_after(t, 0).wait_send()

        @pl.when((block < last) & (t > 0))
        def _():
            pres_after(t, 1).wait_send()

        return carry

    lax.fori_loop(0, steps, sent, 0)

    @pl.when(block > 0)
    def _():
        buoy_before.wait_send()

    @pl.when(block < last)
    def _():
        buoy_after.wait_send()

    lax.fori_loop(1, tiles, gather_wait, 0)


def stacked(table, axis):
    high = table.astype(jnp.bfloat16)
    low = (table - high.astype(np.float64)).astype(jnp.bfloat16)
    return jnp.asarray(np.concatenate([high, high, low], axis=axis))


def block_path(kappa, buoyancy, source_state, traces, panel_tile, rcv_index):
    count, depth_y, depth_z = kappa.shape
    tiles = lax.axis_size("tx")
    extent = count * tiles
    panels, steps, width = traces.shape
    vmem = pl.BlockSpec(memory_space=pltpu.VMEM)
    land, load = pl.pallas_call(
        spread_kernel,
        out_shape=(
            jax.ShapeDtypeStruct((6, extent * ROWS, depth_z), jnp.float32),
            jax.ShapeDtypeStruct((tiles * panels, steps + 1, width), jnp.float32),
        ),
        in_specs=[pl.BlockSpec(memory_space=pltpu.HBM)] * 4
        + [pl.BlockSpec(memory_space=pltpu.SMEM), vmem],
        out_specs=(vmem, vmem),
        scratch_shapes=[
            pltpu.VMEM((6, count, depth_y, depth_z), jnp.float32),
            pltpu.VMEM((panels, steps, width), jnp.float32),
            pltpu.SemaphoreType.DMA((4,)),
            pltpu.SemaphoreType.DMA((2, tiles)),
            pltpu.SemaphoreType.DMA((2, tiles)),
            pltpu.SemaphoreType.DMA((3, tiles, SHARES)),
            pltpu.SemaphoreType.DMA((tiles, SHARES)),
        ],
        compiler_params=pltpu.CompilerParams(
            collective_id=1, has_side_effects=True, vmem_limit_bytes=24 * 1024 * 1024
        ),
    )(kappa, buoyancy, source_state, traces, panel_tile.reshape(-1), rcv_index)
    dense = pl.pallas_call(
        scatter_kernel,
        out_shape=jax.ShapeDtypeStruct((steps, extent, ROWS, depth_z), jnp.float32),
        in_specs=[vmem],
        out_specs=vmem,
        scratch_shapes=[
            pltpu.VMEM((tiles * panels // width, width), jnp.int32),
            pltpu.SMEM((tiles * panels // width, width), jnp.int32),
            pltpu.SemaphoreType.DMA,
        ],
        compiler_params=pltpu.CompilerParams(vmem_limit_bytes=24 * 1024 * 1024),
    )(load)
    dense = dense.reshape(steps, extent * ROWS, depth_z)
    shape = (extent, depth_z)
    out = pl.pallas_call(
        wave_kernel,
        out_shape=jax.ShapeDtypeStruct((2, count, depth_y, depth_z), jnp.float32),
        in_specs=[vmem] * 6,
        out_specs=vmem,
        scratch_shapes=[
            pltpu.VMEM((steps + 1, 2, EXT) + shape, jnp.float32),
            pltpu.VMEM((2, ROWS) + shape, jnp.float32),
            pltpu.VMEM((2, VEXT) + shape, jnp.float32),
            pltpu.VMEM((2, ROWS) + shape, jnp.float32),
            pltpu.VMEM((VEXT,) + shape, jnp.float32),
            pltpu.VMEM((ROWS,) + shape, jnp.float32),
            pltpu.VMEM((2, ROWS) + shape, jnp.float32),
            pltpu.VMEM((ROWS,) + shape, jnp.float32),
            pltpu.VMEM((2, extent * ROWS, depth_z), jnp.float32),
            pltpu.SemaphoreType.DMA((2, 2 * steps + 2)),
            pltpu.SemaphoreType.DMA((2, 2 * steps + 2)),
            pltpu.SemaphoreType.DMA((2, tiles)),
            pltpu.SemaphoreType.DMA((2, tiles)),
        ],
        compiler_params=pltpu.CompilerParams(
            collective_id=0, has_side_effects=True, vmem_limit_bytes=40 * 1024 * 1024
        ),
    )(
        land,
        dense,
        stacked(spectral_matrix(extent, 0), 1),
        stacked(spectral_matrix(extent, 1), 1),
        stacked(line_matrix(depth_z, True), 0),
        stacked(line_matrix(depth_z, False), 0),
    )
    return (out[0], out[1])


def on_device(kappa, buoyancy, source_state, traces, panel_tile, rcv_index):
    count, depth_y, depth_z = kappa.shape
    tiles = lax.axis_size("tx")
    extent = count * tiles
    fits = depth_y == ROWS * tiles and depth_z == 128 and traces.shape[2] == 128
    fits = fits and count == 2 and tiles % 4 == 0 and extent % 16 == 0
    fits = fits and extent * depth_y * depth_z <= 1 << 24
    fits = fits and traces.shape[0] * tiles % 128 == 0 and traces.shape[0] % 4 == 0
    path = block_path if fits else transposed_path
    return path(kappa, buoyancy, source_state, traces, panel_tile, rcv_index)


def solution(mesh):
    return jax.shard_map(
        on_device,
        mesh=mesh,
        in_specs=(
            P("tx", None, None),
            P("tx", None, None),
            P(None, ("shots", "tx"), None, None),
            P(("shots", "tx"), None, None),
            P(("shots", "tx"), None),
            P(("shots", "tx"), None),
        ),
        out_specs=(P(("shots", "tx"), None, None), P(("shots", "tx"), None, None)),
        check_vma=False,
    )
```
